32 devices in a mesh: clip: 2 (over x), gz: 16 (over z, y, core).
Axes of the slice: x: 2, y: 2, z: 4, core: 2. Of those that a mesh axis runs over, the one named last changes fastest.
Arguments:
- source_term: float32 [2, 128, 64, 128], P(None, ('clip', 'gz')), parts along dimension 1, may hold values from -24 to 24
- material: int32 [128, 64, 128], P(('clip', 'gz')), parts along dimension 0, may hold values from 0 to 2
- orders: int32 [2, 1024], P(None, 'gz'), may hold values from -22 to 22
Outputs:
- solution: float32 [2, 128, 64, 128], P(None, ('clip', 'gz')), parts along dimension 1
- residual: float32 [2, 128, 64, 128], P(None, ('clip', 'gz')), parts along dimension 1
- pupil_orders: float32 [2, 2048], P(None, ('clip', 'gz')), parts along dimension 1
The draws below stay inside these ranges and needn't reach their ends.
There are 2 independent parts, one for each index of `clip`. The reference program is written for one: setup_inputs(seed, part) draws one part's arguments, and reference() takes and returns one part's arrays. A program takes and returns all parts, laid end to end along the dimension named above; an argument that names none is the same for every part. Nothing has to cross between parts.
All inputs are finite; a program needn't handle non-finite values.
Results may differ from the reference program's by a relative error of at most 0.0003.
Values sent between devices are 32-bit elements; how exact they have to be, the bound alone decides.
No kernel may reach another device: no remote copies, remote signals or barrier semaphores. Data moves between devices by JAX's collectives and lax.ppermute only.
A program may use at most 128 MiB of HBM per device.

```python
import math
import jax
import jax.numpy as jnp
from jax import lax

NX = 64
NY = 128
LEVELS = 3
SWEEPS = 2
COARSE_SWEEPS = 4
ORD_HALF = 22
ORDERS = 1024
NZ = 64


def draw_source_term(key, part):
    planes = jnp.arange(NZ, dtype=jnp.float32)
    profile = 1.0 + 2.0 * planes / max(NZ - 1, 1)
    profile = profile[None, :, None, None]
    base = 2.0 * jnp.clip(jax.random.normal(key, (2, NZ, NX, NY), jnp.float32), -4.0, 4.0)
    return base * profile


def touch_ends(entries, key, smallest, high):
    longest = entries.shape.index(max(entries.shape))
    spots = []
    for shift in (0, 1):
        where = [jax.random.randint(jax.random.fold_in(key, axis), (), 0, length) for axis, length in enumerate(entries.shape)]
        where[longest] = (where[longest] + shift) % entries.shape[longest]
        spots.append(tuple(where))
    return entries.at[spots[0]].set(smallest).at[spots[1]].set(high)


def setup_inputs(seed: int = 0, part: int = 0) -> dict:
    streams_of = jax.random.split(jax.random.key(seed), 4)
    own_keys = jax.random.split(jax.random.fold_in(streams_of[3], part), 4)
    return {
        "source_term": draw_source_term(jax.random.fold_in(jax.random.fold_in(streams_of[3], part), 71), part),
        "material": touch_ends(jax.random.randint(own_keys[1], (NZ, NX, NY), 0, 3), jax.random.fold_in(own_keys[1], 1), 0, 2).astype(jnp.int32),
        "orders": touch_ends(jax.random.randint(streams_of[2], (2, ORDERS), 0 - ORD_HALF, ORD_HALF + 1), jax.random.fold_in(streams_of[2], 1), 0 - ORD_HALF, ORD_HALF).astype(jnp.int32),
    }


HELM_TABLE = ((-0.5, 0.0), (1.0, -1.4), (-1.2, 0.0))
SHIFT_TABLE = ((-0.5, -0.25), (1.0, -0.25 * math.sqrt(11.84)), (-1.2, -0.6))
RELAX_WEIGHT = 0.8

def lookup(material, lookup_table):
    columns = []
    for member in range(2):
        chosen = jnp.where(material == 1, lookup_table[1][member], jnp.where(material == 2, lookup_table[2][member], lookup_table[0][member]))
        columns.append(chosen.astype(jnp.float32))
    return jnp.stack(columns)

def complex_mul(left_side, right_side):
    return jnp.stack([left_side[0] * right_side[0] - left_side[1] * right_side[1], left_side[0] * right_side[1] + left_side[1] * right_side[0]])

def divide_by(numer_real, numer_imag, denom_real, denom_imag):
    modulus = denom_real * denom_real + denom_imag * denom_imag
    return jnp.stack([(numer_real * denom_real + numer_imag * denom_imag) / modulus, (numer_imag * denom_real - numer_real * denom_imag) / modulus])

def neighbours(padded):
    middle = padded[:, 1:-1]
    summed = padded[:, 2:] + padded[:, :-2]
    summed = summed + jnp.roll(middle, 1, axis=2) + jnp.roll(middle, -1, axis=2)
    summed = summed + jnp.roll(middle, 1, axis=3) + jnp.roll(middle, -1, axis=3)
    return summed

def operate(padded, coefficient, factor):
    middle = padded[:, 1:-1]
    return (6.0 * middle - neighbours(padded)) * factor + complex_mul(coefficient, middle)

def inverse_diagonal(shift_field, factor):
    diag_real = 6.0 * factor + shift_field[0]
    diag_imag = shift_field[1]
    modulus = diag_real * diag_real + diag_imag * diag_imag
    return jnp.stack([diag_real / modulus, -diag_imag / modulus])

def pad_planes(values):
    return jnp.pad(values, ((0, 0), (1, 1), (0, 0), (0, 0)))

def restrict(values):
    planes, height, breadth = (values.shape[1], values.shape[2], values.shape[3])
    blocks = values.reshape(2, planes // 2, 2, height // 2, 2, breadth // 2, 2)
    return lax.optimization_barrier(jnp.mean(blocks, axis=(2, 4, 6)))

def prolong(values):
    for which_axis in (1, 2, 3):
        values = jnp.repeat(values, 2, axis=which_axis)
    return values

def relax_once(values, source, shift_field, inverse, factor, padded):
    remainder = source - operate(padded, shift_field, factor)
    return values + RELAX_WEIGHT * complex_mul(inverse, remainder)

def multigrid_cycle(source, shifts, inverses, grid_level):
    factor = 0.25 ** grid_level
    shift_field = shifts[grid_level]
    inverse = inverses[grid_level]
    values = RELAX_WEIGHT * complex_mul(inverse, source)
    if grid_level == LEVELS - 1:
        for sweep_index in range(COARSE_SWEEPS - 1):
            values = relax_once(values, source, shift_field, inverse, factor, pad_planes(values))
        return values
    for sweep_index in range(SWEEPS - 1):
        values = relax_once(values, source, shift_field, inverse, factor, pad_planes(values))
    remainder = source - operate(pad_planes(values), shift_field, factor)
    coarse = multigrid_cycle(restrict(remainder), shifts, inverses, grid_level + 1)
    values = values + prolong(coarse)
    for sweep_index in range(SWEEPS):
        values = relax_once(values, source, shift_field, inverse, factor, pad_planes(values))
    return values

def precise_dot(left_side, right_side):
    return jnp.dot(left_side, right_side, precision=lax.Precision.HIGHEST, preferred_element_type=jnp.float32)

def phase_table(length):
    positions = jnp.arange(length, dtype=jnp.int32)
    harmonics = jnp.arange(2 * ORD_HALF + 1, dtype=jnp.int32) - ORD_HALF
    phase_index = positions[:, None] * harmonics[None, :] % length
    angles = phase_index.astype(jnp.float32) * (2.0 * math.pi / length)
    return (jnp.cos(angles), -jnp.sin(angles))

def spectrum_of(plane):
    height = plane.shape[1]
    breadth = plane.shape[2]
    cos_x, sin_x = phase_table(height)
    cos_y, sin_y = phase_table(breadth)
    inner_real = precise_dot(plane[0], cos_y) - precise_dot(plane[1], sin_y)
    inner_imag = precise_dot(plane[0], sin_y) + precise_dot(plane[1], cos_y)
    outer_real = precise_dot(cos_x.T, inner_real) - precise_dot(sin_x.T, inner_imag)
    outer_imag = precise_dot(cos_x.T, inner_imag) + precise_dot(sin_x.T, inner_real)
    return jnp.stack([outer_real, outer_imag]) * (1.0 / math.sqrt(height * breadth))

def reference(source_term, material, orders):
    helm_coef = lookup(material, HELM_TABLE)
    shifts = [lookup(material, SHIFT_TABLE)]
    for grid_level in range(1, LEVELS):
        shifts.append(restrict(shifts[-1]))
    inverses = [inverse_diagonal(shifts[grid_level], 0.25 ** grid_level) for grid_level in range(LEVELS)]
    norm_sum = jnp.sum(source_term * source_term)
    direction = multigrid_cycle(source_term, shifts, inverses, 0)
    image_field = operate(pad_planes(direction), helm_coef, 1.0)
    cross_real = jnp.sum(source_term[0] * image_field[0] + source_term[1] * image_field[1])
    cross_imag = jnp.sum(source_term[0] * image_field[1] - source_term[1] * image_field[0])
    step_alpha = divide_by(norm_sum, 0.0, cross_real, cross_imag)
    halfway = source_term - complex_mul(step_alpha, image_field)
    corrected = multigrid_cycle(halfway, shifts, inverses, 0)
    last_image = operate(pad_planes(corrected), helm_coef, 1.0)
    along_real = jnp.sum(last_image[0] * halfway[0] + last_image[1] * halfway[1])
    along_imag = jnp.sum(last_image[0] * halfway[1] - last_image[1] * halfway[0])
    image_norm = jnp.sum(last_image * last_image)
    step_omega = divide_by(along_real, along_imag, image_norm, 0.0)
    solution = complex_mul(step_alpha, direction) + complex_mul(step_omega, corrected)
    residual = halfway - complex_mul(step_omega, last_image)
    spectrum = spectrum_of(solution[:, -1])
    pupil_orders = spectrum[:, orders[0] + ORD_HALF, orders[1] + ORD_HALF]
    return (solution, residual, pupil_orders)
```

```python
import functools
import math

import jax
import jax.numpy as jnp
import numpy as np
from jax import lax
from jax.experimental import pallas as pl
from jax.experimental.pallas import tpu as pltpu
from jax.sharding import PartitionSpec as P

ORD_HALF = 22
HELM_TABLE = ((-0.5, 0.0), (1.0, -1.4), (-1.2, 0.0))
SHIFT_TABLE = ((-0.5, -0.25), (1.0, -0.25 * math.sqrt(11.84)), (-1.2, -0.6))
RELAX = 0.8
KEEP = 1.0 - RELAX
PLANES = 4
OWN = 2 * PLANES
WINDOW = 5 * PLANES
PAD1 = 8
PAD2 = 4
H1 = 0.25
H2 = 0.0625
F32 = jnp.float32

WEIGHTS = tuple(RELAX / complex(6.0 + s[0], s[1]) for s in SHIFT_TABLE)


def pick(code, values):
    return jnp.where(
        code == 1.0,
        values[0],
        jnp.where(code == 2.0, values[1], jnp.where(code == 3.0, values[2], 0.0)),
    )


def weight_of(code):
    return pick(code, [w.real for w in WEIGHTS]), pick(code, [w.imag for w in WEIGHTS])


def shift_of(code):
    return pick(code, [s[0] for s in SHIFT_TABLE]), pick(code, [s[1] for s in SHIFT_TABLE])


def helm_of(code):
    return pick(code, [s[0] for s in HELM_TABLE]), pick(code, [s[1] for s in HELM_TABLE])


def cmul(ar, ai, br, bi):
    return ar * br - ai * bi, ar * bi + ai * br


def around(ref, p, lead=()):
    sums = []
    for c in range(2):
        mid = ref[c, p]
        nx, ny = mid.shape
        total = ref[c, p - 1] + ref[c, p + 1]
        total = total + pltpu.roll(mid, 1, 0) + pltpu.roll(mid, nx - 1, 0)
        total = total + pltpu.roll(mid, 1, 1) + pltpu.roll(mid, ny - 1, 1)
        sums.append(total)
    return sums


def lanes(shape):
    return lax.broadcasted_iota(jnp.int32, shape, len(shape) - 1)


def around_packed(ref, p, part):
    mid = ref[p]
    n = mid.shape[0]
    width = mid.shape[1]
    total = ref[p - 1] + ref[p + 1]
    total = total + pltpu.roll(mid, 1, 0) + pltpu.roll(mid, n - 1, 0)
    at = lanes(mid.shape) % part
    before = jnp.where(at == 0, pltpu.roll(mid, width + 1 - part, 1), pltpu.roll(mid, 1, 1))
    after = jnp.where(at == part - 1, pltpu.roll(mid, part - 1, 1), pltpu.roll(mid, width - 1, 1))
    return total + before + after


def cmul_packed(wr, wi, g, part):
    return wr * g + wi * pltpu.roll(g, part, 1)


def weights_packed(shift, part, factor):
    other = pltpu.roll(shift, part, 1)
    real_lane = lanes(shift.shape) % (2 * part) < part
    dr = 6.0 * factor + jnp.where(real_lane, shift, other)
    di = jnp.where(real_lane, other, shift)
    scale = RELAX / (dr * dr + di * di)
    wi = -di * scale
    return dr * scale, jnp.where(real_lane, -wi, wi)


def dot(a, b):
    return jnp.dot(a, b, precision=lax.Precision.HIGHEST, preferred_element_type=F32)


def iota2(rows, cols):
    return (
        lax.broadcasted_iota(jnp.int32, (rows, cols), 0),
        lax.broadcasted_iota(jnp.int32, (rows, cols), 1),
    )


def restrict_fine(real, imag, tmp):
    nx, ny = real.shape
    tmp[0] = real
    tmp[1] = imag
    half = nx // 2
    rows = [tmp[c, pl.ds(0, half, stride=2), :] + tmp[c, pl.ds(1, half, stride=2), :] for c in range(2)]
    r, c = iota2(2 * ny, ny)
    pool = jnp.where(r // 2 == c, 0.125, 0.0).astype(F32)
    return dot(jnp.concatenate(rows, axis=1), pool)


def each(lower, upper, body):
    def step(p, carry):
        body(p)
        return carry

    lax.fori_loop(lower, upper, step, 0)


def full(shape_dtype):
    return jax.ShapeDtypeStruct(shape_dtype, F32)


VM = pl.BlockSpec(memory_space=pltpu.VMEM)
SM = pl.BlockSpec(memory_space=pltpu.SMEM)


def call(body, outs, inputs, scratch, name):
    size = sum(4 * math.prod(x.shape) for x in inputs) + sum(4 * math.prod(o) for o in outs)
    return pl.pallas_call(
        body,
        out_shape=[full(o) for o in outs],
        in_specs=[SM] + [VM] * (len(inputs) - 1),
        out_specs=[VM] * len(outs),
        scratch_shapes=[pltpu.VMEM(s, F32) for s in scratch],
        cost_estimate=pl.CostEstimate(flops=40 * size, bytes_accessed=size, transcendentals=0),
        name=name,
    )(*inputs)


def first_kernel(at, own, near, swap, orders, out, u, e1, u2, tmp):
    odd = at[1]

    def fill(block, first):
        def body(p):
            code = block[2, p]
            wr, wi = weight_of(code)
            ur, ui = cmul(wr, wi, block[0, p], block[1, p])
            u[0, first + p] = ur
            u[1, first + p] = ui

        each(0, PLANES, body)

    fill(own, PLANES)
    fill(near, 2 * PLANES - 2 * PLANES * odd)
    fill(swap, 2 * PLANES * odd)

    def smooth(p, block, q):
        sr, si = around(u, p)
        er = KEEP * block[0, q] + sr
        ei = KEEP * block[1, q] + si
        wr, wi = weight_of(block[2, q])
        vr, vi = cmul(wr, wi, er, ei)
        u2[0, p] = vr
        u2[1, p] = vi
        return er, ei

    def inner(q):
        er, ei = smooth(PLANES + q, own, q)
        e1[0, q] = er
        e1[1, q] = ei

    each(0, PLANES, inner)

    @pl.when(odd == 0)
    def _():
        smooth(PLANES - 1, swap, PLANES - 1)
        smooth(2 * PLANES, near, 0)

    @pl.when(odd == 1)
    def _():
        smooth(PLANES - 1, near, PLANES - 1)
        smooth(2 * PLANES, swap, 0)

    half = own.shape[2] // 2
    for q in range(PLANES // 2):
        total = [0.0, 0.0, 0.0, 0.0]
        for k in range(2):
            p = 2 * q + k
            s = around(u2, PLANES + p)
            shift = shift_of(own[2, p])
            for c in range(2):
                total[c] = total[c] + KEEP * e1[c, p] + s[c]
                total[2 + c] = total[2 + c] + shift[c]
        out[pl.ds(half * q, half), :] = restrict_fine(total[0], total[1], tmp)
        out[pl.ds(half * (2 + q), half), :] = restrict_fine(total[2], total[3], tmp)
    out[pl.ds(4 * half, 8), :] = jnp.broadcast_to(orders[...], (8, orders.shape[1]))


def coarse_shapes(group, nx, ny):
    n1 = (2 * group + 2 * PAD1, nx // 2, ny)
    n2 = (group + 2 * PAD2, nx // 4, ny)
    return [n1] * 5 + [n2] * 3 + [(nx // 2, ny)]


def coarse_weights(me, masks, pieces, w1r, w1i, w2r, w2i, shift2, tmp):
    half, ny = tmp.shape
    group = len(masks)
    for ref, pad in ((w1r, PAD1), (w1i, PAD1), (w2r, PAD2), (w2i, PAD2)):
        zero = jnp.zeros(ref.shape[1:], F32)
        for k in range(pad):
            ref[k] = zero
            ref[ref.shape[0] - 1 - k] = zero
    for mask, (piece, j) in zip(masks, pieces, strict=True):
        d = me ^ mask
        planes = [piece[j, pl.ds(half * (2 + k), half), :] for k in range(2)]
        for k in range(2):
            wr, wi = weights_packed(planes[k], ny // 2, H1)
            w1r[PAD1 + 2 * d + k] = wr
            w1i[PAD1 + 2 * d + k] = wi
        tmp[...] = planes[0] + planes[1]
        shift2[d] = tmp[pl.ds(0, half // 2, stride=2), :] + tmp[pl.ds(1, half // 2, stride=2), :]
    flat = shift2[...].reshape(group * (half // 2), ny)
    s2 = dot(flat, pool_level1(ny)).reshape(group, half // 2, ny)
    for d in range(group):
        wr, wi = weights_packed(s2[d], ny // 4, H2)
        w2r[PAD2 + d] = wr
        w2i[PAD2 + d] = wi


def pool_level1(ny):
    r, c = iota2(ny, ny)
    return jnp.where(r // 2 == c % (ny // 2), 0.125, 0.0).astype(F32)


def coarse_solve(me, masks, pieces, reach, w1r, w1i, w2r, w2i, g1, u1, e1, u2, v1, g2, va, vb, tmp, out):
    half, ny = tmp.shape
    group = len(masks)
    part1, part2 = ny // 2, ny // 4
    n1 = 2 * group
    for ref, pad in ((g1, PAD1), (u1, PAD1), (u2, PAD1), (v1, PAD1), (va, PAD2), (vb, PAD2)):
        zero = jnp.zeros(ref.shape[1:], F32)
        for k in range(pad):
            ref[k] = zero
            ref[ref.shape[0] - 1 - k] = zero
    for mask, (piece, j) in zip(masks, pieces, strict=True):
        d = me ^ mask
        for k in range(2):
            p = PAD1 + 2 * d + k
            g = piece[j, pl.ds(half * k, half), :]
            g1[p] = g
            u1[p] = cmul_packed(w1r[p], w1i[p], g, part1)

    def pre(p):
        e = KEEP * g1[p] + H1 * around_packed(u1, p, part1)
        u = cmul_packed(w1r[p], w1i[p], e, part1)
        e1[p] = e
        u2[p] = u
        v1[p] = u1[p] + u

    each(PAD1, PAD1 + n1, pre)

    def coarser(d):
        total = 0.0
        for k in range(2):
            p = PAD1 + 2 * d + k
            total = total + KEEP * e1[p] + H1 * around_packed(u2, p, part1)
        tmp[...] = total
        g2[PAD2 + d] = tmp[pl.ds(0, half // 2, stride=2), :] + tmp[pl.ds(1, half // 2, stride=2), :]

    each(0, group, coarser)
    flat = g2[pl.ds(PAD2, group)].reshape(group * (half // 2), ny)
    r2 = dot(flat, pool_level1(ny)).reshape(group, half // 2, ny)
    for d in range(group):
        g2[PAD2 + d] = r2[d]
        va[PAD2 + d] = cmul_packed(w2r[PAD2 + d], w2i[PAD2 + d], r2[d], part2)
    for src, dst in ((va, vb), (vb, va), (va, vb)):

        def sweep(p, src=src, dst=dst):
            s = g2[p] + H2 * around_packed(src, p, part2)
            dst[p] = KEEP * src[p] + cmul_packed(w2r[p], w2i[p], s, part2)

        each(PAD2, PAD2 + group, sweep)
    reach2 = (reach + 2) // 2
    count = 2 * reach2 + 1
    first2 = PAD2 + me - reach2
    flat = vb[pl.ds(first2, count)].reshape(count * (half // 2), ny)
    r, c = iota2(ny, ny)
    spread = jnp.where(c // 2 == r, 1.0, 0.0).astype(F32)
    e2 = dot(flat, spread).reshape(count, half // 2, ny)
    base = PAD1 + 2 * (me - reach2)
    for k in range(count):
        tmp[pl.ds(0, half // 2, stride=2), :] = e2[k]
        tmp[pl.ds(1, half // 2, stride=2), :] = e2[k]
        add = tmp[...]
        v1[base + 2 * k] = v1[base + 2 * k] + add
        v1[base + 2 * k + 1] = v1[base + 2 * k + 1] + add

    def post(src, p):
        s = g1[p] + H1 * around_packed(src, p, part1)
        return KEEP * src[p] + cmul_packed(w1r[p], w1i[p], s, part1)

    start = PAD1 + 2 * me

    def third(p):
        u1[p] = post(v1, p)

    def fourth(k):
        out[k] = post(u1, start - reach + k)

    each(start - reach - 1, start + reach + 3, third)
    each(0, 2 * reach + 2, fourth)


def add_correction(ec, v, tmp, planes):
    half, ny = ec.shape[1:]
    r, c = iota2(ny, 2 * ny)
    spread = jnp.where(c // 2 == r, 1.0, 0.0).astype(F32)

    def body(k):
        both = dot(ec[k], spread)
        for c in range(2):
            e = both[:, c * ny : (c + 1) * ny]
            tmp[c, pl.ds(0, half, stride=2), :] = e
            tmp[c, pl.ds(1, half, stride=2), :] = e
            add = tmp[c]
            v[c, 2 * k] = v[c, 2 * k] + add
            v[c, 2 * k + 1] = v[c, 2 * k + 1] + add

    each(0, planes, body)


def second_kernel(
    masks, layout, at, own, near, swap, skip, far, *refs
):
    n = max(i for i, _ in layout) + 1
    gathered, refs = refs[:n], refs[n:]
    (direction, image, smooth2, weight, pay, w1r, w1i, w2r, w2i), refs = refs[:9], refs[9:]
    f, u, u2, v, code, tmp, ec, e1, shift2 = refs[:9]
    coarse = refs[9:]
    me, odd = at[0], at[1]
    pieces = [(gathered[i], j) for i, j in layout]

    def fill(block, first):
        def body(q):
            p = first + q
            c = block[2, q]
            wr, wi = weight_of(c)
            fr, fi = block[0, q], block[1, q]
            ur, ui = cmul(wr, wi, fr, fi)
            f[0, p], f[1, p] = fr, fi
            weight[0, p], weight[1, p] = wr, wi
            u[0, p], u[1, p] = ur, ui
            code[p] = c

        each(0, PLANES, body)

    fill(own, OWN)
    fill(near, OWN + PLANES - 2 * PLANES * odd)
    fill(swap, OWN - PLANES + 2 * PLANES * odd)
    fill(skip, 4 * PLANES * odd)
    fill(far, 4 * PLANES - 4 * PLANES * odd)

    def pre(p):
        sr, si = around(u, p)
        vr, vi = cmul(weight[0, p], weight[1, p], KEEP * f[0, p] + sr, KEEP * f[1, p] + si)
        v[0, p] = u[0, p] + vr
        v[1, p] = u[1, p] + vi

    each(1, WINDOW - 1, pre)
    coarse_weights(me, masks, pieces, w1r, w1i, w2r, w2i, shift2, coarse[-1])
    coarse_solve(me, masks, pieces, 4, w1r, w1i, w2r, w2i, *coarse, ec)
    add_correction(ec, v, tmp, WINDOW // 2)

    def sweep(src, dst, p):
        sr, si = around(src, p)
        vr, vi = cmul(weight[0, p], weight[1, p], f[0, p] + sr, f[1, p] + si)
        dst[0, p] = KEEP * src[0, p] + vr
        dst[1, p] = KEEP * src[1, p] + vi

    each(2, WINDOW - 2, lambda p: sweep(v, u, p))
    each(3, WINDOW - 3, lambda p: sweep(u, v, p))

    def apply(p):
        sr, si = around(v, p)
        c = code[p]
        hr, hi = helm_of(c)
        vr, vi = v[0, p], v[1, p]
        ar, ai = cmul(hr, hi, vr, vi)
        ar = jnp.where(c > 0.0, ar + 6.0 * vr - sr, 0.0)
        ai = jnp.where(c > 0.0, ai + 6.0 * vi - si, 0.0)
        image[0, p - 4] = ar
        image[1, p - 4] = ai
        ur, ui = cmul(weight[0, p], weight[1, p], ar, ai)
        u[0, p] = ur
        u[1, p] = ui

    each(4, WINDOW - 4, apply)
    nx = own.shape[2]
    rho, cross_r, cross_i = 0.0, 0.0, 0.0
    for q in range(PLANES):
        fr, fi = own[0, q], own[1, q]
        ir, ii = image[0, OWN - 4 + q], image[1, OWN - 4 + q]
        rho = rho + fr * fr + fi * fi
        cross_r = cross_r + fr * ir + fi * ii
        cross_i = cross_i + fr * ii - fi * ir
        for c in range(2):
            direction[c, q] = v[c, OWN + q]
    half = nx // 2
    row = lax.broadcasted_iota(jnp.int32, (8, own.shape[3]), 0)
    sums = [jnp.sum(t, axis=0, keepdims=True) for t in (rho, cross_r, cross_i)]
    tail = jnp.where(row == 0, sums[0], jnp.where(row == 1, sums[1], jnp.where(row == 2, sums[2], 0.0)))
    pay[pl.ds(2 * half, 8), :] = tail

    def pre2(p):
        sr, si = around(u, p)
        er = KEEP * image[0, p - 4] + sr
        ei = KEEP * image[1, p - 4] + si
        vr, vi = cmul(weight[0, p], weight[1, p], er, ei)
        e1[0, p], e1[1, p] = er, ei
        u2[0, p], u2[1, p] = vr, vi
        smooth2[0, p - 5] = u[0, p] + vr
        smooth2[1, p - 5] = u[1, p] + vi

    each(5, WINDOW - 5, pre2)
    for q in range(PLANES // 2):
        total = [0.0, 0.0]
        for k in range(2):
            p = OWN + 2 * q + k
            s = around(u2, p)
            for c in range(2):
                total[c] = total[c] + KEEP * e1[c, p] + s[c]
        pay[pl.ds(half * q, half), :] = restrict_fine(total[0], total[1], tmp)


def phase_kernel(masks, layout, row, at, *refs):
    n = max(i for i, _ in layout) + 1
    gathered = refs[:n]
    table, qrow, found = refs[n:]
    me = at[0]
    ny = found.shape[1]
    nx = table.shape[0] // 2
    for mask, (i, j) in zip(masks, layout, strict=True):
        found[pl.ds(me ^ mask, 1), :] = gathered[i][j, pl.ds(row, 1), :]
    low = lanes((1, ny)) < ny // 2
    x = lax.broadcasted_iota(jnp.int32, (nx, ny), 0)
    for pair in range(len(masks) // 2):
        even = found[pl.ds(2 * pair, 1), :]
        odd = found[pl.ds(2 * pair + 1, 1), :]
        p = jnp.where(low, even, pltpu.roll(odd, ny // 2, 1))
        q = jnp.where(low, pltpu.roll(even, ny // 2, 1), odd)
        turns = (x * p.astype(jnp.int32)) & (nx - 1)
        angle = turns.astype(F32) * (2.0 * math.pi / nx)
        table[pl.ds(0, nx), pl.ds(pair * ny, ny)] = jnp.cos(angle)
        table[pl.ds(nx, nx), pl.ds(pair * ny, ny)] = -jnp.sin(angle)
        qrow[:, pl.ds(pair * ny, ny)] = jnp.broadcast_to(q, (8, ny))


def third_kernel(
    masks, layout, at, own, direction, image, smooth2, weight, w1r, w1i, w2r, w2i, ytable, xtable, qrow, *refs
):
    n = max(i for i, _ in layout) + 1
    gathered, refs = refs[:n], refs[n:]
    (corrected, last_image, halfway, pay, alpha), refs = refs[:5], refs[5:]
    u, v, tmp, ec = refs[:4]
    coarse = refs[4:]
    me = at[0]
    pieces = [(gathered[i], j) for i, j in layout]
    nx, ny = own.shape[2:]
    half = nx // 2
    coarse_solve(me, masks, pieces, 2, w1r, w1i, w2r, w2i, *coarse, ec)

    def take(p):
        v[0, p] = smooth2[0, p - 1]
        v[1, p] = smooth2[1, p - 1]

    each(1, 11, take)
    add_correction(ec, v, tmp, 6)

    def sweep(src, dst, p):
        sr, si = around(src, p)
        w = p + OWN - 4
        vr, vi = cmul(weight[0, w], weight[1, w], image[0, p] + sr, image[1, p] + si)
        dst[0, p] = KEEP * src[0, p] + vr
        dst[1, p] = KEEP * src[1, p] + vi

    each(2, 10, lambda p: sweep(v, u, p))
    each(3, 9, lambda p: sweep(u, v, p))

    sums = 0.0
    for i, j in layout:
        sums = sums + gathered[i][j, pl.ds(2 * half, 8), :]
    rho, cr, ci = [jnp.sum(sums[k : k + 1], axis=1, keepdims=True) for k in range(3)]
    modulus = cr * cr + ci * ci
    ar = rho * cr / modulus
    ai = -rho * ci / modulus
    dots = [0.0, 0.0, 0.0]
    for q in range(PLANES):
        p = 4 + q
        sr, si = around(v, p)
        hr, hi = helm_of(own[2, q])
        wr, wi = v[0, p], v[1, p]
        br, bi = cmul(hr, hi, wr, wi)
        br, bi = br + 6.0 * wr - sr, bi + 6.0 * wi - si
        ir, ii = image[0, p], image[1, p]
        br, bi = cmul(ar, ai, br, bi)
        lr, li = ir - br, ii - bi
        tr, ti = cmul(ar, ai, ir, ii)
        hr, hi = own[0, q] - tr, own[1, q] - ti
        xr, xi = cmul(ar, ai, wr, wi)
        corrected[0, q], corrected[1, q] = direction[0, q] - xr, direction[1, q] - xi
        last_image[0, q], last_image[1, q] = lr, li
        halfway[0, q], halfway[1, q] = hr, hi
        dots[0] = dots[0] + lr * hr + li * hi
        dots[1] = dots[1] + lr * hi - li * hr
        dots[2] = dots[2] + lr * lr + li * li
    dots = [jnp.sum(t, axis=0, keepdims=True) for t in dots]
    row = lax.broadcasted_iota(jnp.int32, (8, ny), 0)
    alpha[...] = jnp.where(row == 0, ar, ai)

    sign = jnp.where(lanes((nx, ny)) < ny // 2, -1.0, 1.0)
    stacked = []
    for field in (direction, corrected):
        plane = field[:, PLANES - 1].reshape(2 * nx, ny)
        m = lax.dot_general(
            ytable[...],
            plane,
            (((1,), (1,)), ((), ())),
            precision=lax.Precision.HIGHEST,
            preferred_element_type=F32,
        )
        t = m[:nx] + sign * pltpu.roll(m[nx:], nx, 1)
        stacked += [-sign * t, pltpu.roll(t, nx, 1)]
    spectrum = dot(jnp.concatenate(stacked, axis=0), xtable[...])
    scale = 1.0 / math.sqrt(nx * ny)
    at_row = lax.broadcasted_iota(jnp.int32, (nx, ny), 0).astype(F32) - ORD_HALF
    for pair in range(len(masks) // 2):
        chosen = at_row == qrow[0:1, pair * ny : (pair + 1) * ny]
        found = [
            scale * jnp.sum(jnp.where(chosen, spectrum[k * nx : (k + 1) * nx, pair * ny : (pair + 1) * ny], 0.0), axis=0, keepdims=True)
            for k in range(4)
        ]
        block = 0.0
        for k, line in enumerate(found + dots):
            block = jnp.where(row == k, line, block)
        pay[2 * pair] = block
        pay[2 * pair + 1] = block


def last_kernel(at, direction, corrected, last_image, halfway, alpha, got, solution, residual, pupil):
    group = got.shape[0]
    ny = got.shape[2]
    total = got[0]
    for k in range(1, group):
        total = total + got[k]
    along_r, along_i, norm = [jnp.sum(total[k : k + 1], axis=1, keepdims=True) for k in (4, 5, 6)]
    wr = along_r / norm
    wi = along_i / norm
    ar = alpha[0:1, 0:1]
    ai = alpha[1:2, 0:1]
    for q in range(PLANES):
        xr, xi = cmul(ar, ai, direction[0, q], direction[1, q])
        yr, yi = cmul(wr, wi, corrected[0, q], corrected[1, q])
        solution[0, q], solution[1, q] = xr + yr, xi + yi
        zr, zi = cmul(wr, wi, last_image[0, q], last_image[1, q])
        residual[0, q], residual[1, q] = halfway[0, q] - zr, halfway[1, q] - zi
    tip = got[group - 1]
    xr, xi = cmul(ar, ai, tip[0:1], tip[1:2])
    yr, yi = cmul(wr, wi, tip[2:3], tip[3:4])
    both = jnp.concatenate([xr + yr, xi + yi], axis=0)
    both = jnp.where(at[1] == 1, pltpu.roll(jnp.broadcast_to(jnp.concatenate([both] * 4, axis=0), (8, ny)), ny // 2, 1)[:2], both)
    pupil[...] = both[:, : ny // 2]


def exchange(x, mask, group):
    return lax.ppermute(x, "gz", [(i, i ^ mask) for i in range(group)])


def swap_across(x, group):
    pairs = []
    for i in range(1, group - 1, 2):
        pairs += [(i, i + 1), (i + 1, i)]
    return lax.ppermute(x, "gz", pairs)


def skip_across(x, group):
    pairs = []
    for i in range(group):
        target = i + 2 if i % 2 == 0 else i - 2
        if 0 <= target < group:
            pairs.append((i, target))
    return lax.ppermute(x, "gz", pairs)


def stages_of(group):
    stages = [[1]]
    stride = 2
    left = group // 2
    if left.bit_length() % 2 == 0:
        stages.insert(0, [stride])
        stride, left = 2 * stride, left // 2
    while left > 1:
        stages.insert(0, [stride, 2 * stride, 3 * stride])
        stride, left = 4 * stride, left // 4
    return stages


def gather(x, group):
    have, masks = x[None], [0]
    stages = stages_of(group)
    for masks_now in stages[:-1]:
        got = [exchange(have, m, group) for m in masks_now]
        masks = masks + [k ^ m for m in masks_now for k in masks]
        have = jnp.concatenate([have] + got, axis=0)
    (m,) = stages[-1]
    other = exchange(have, m, group)
    count = len(masks)
    layout = [(0, j) for j in range(count)] + [(1, j) for j in range(count)]
    return [have, other], masks + [k ^ m for k in masks], layout


def y_phases(nx, ny):
    q = np.arange(nx) - ORD_HALF
    turns = (q[:, None] * np.arange(ny)[None, :]) % ny
    angle = turns.astype(np.float64) * (2.0 * np.pi / ny)
    return np.concatenate([np.cos(angle), -np.sin(angle)], axis=0).astype(np.float32)


def on_device(source_term, material, orders):
    group = lax.axis_size("gz")
    _, planes, nx, ny = source_term.shape
    assert planes == PLANES and 2 * nx == ny and 2 * orders.shape[1] == ny
    me = lax.axis_index("gz")
    at = jnp.stack([me, me % 2]).astype(jnp.int32)
    half = nx // 2

    own = jnp.concatenate([source_term, (material + 1).astype(F32)[None]], axis=0)
    near = exchange(own, 1, group)
    swap = swap_across(own, group)
    order_row = orders.astype(F32).reshape(1, ny)
    fine = (2, PLANES, nx, ny)
    (pay1,) = call(
        first_kernel,
        [(4 * half + 8, ny)],
        [at, own, near, swap, order_row],
        [(2, 3 * PLANES, nx, ny), fine, (2, 3 * PLANES, nx, ny), (2, nx, ny)],
        "first",
    )
    gathered1, masks, layout = gather(pay1, group)
    skip = skip_across(own, group)
    far = exchange(swap, 1, group)

    window = (2, WINDOW, nx, ny)
    shapes1 = (2 * group + 2 * PAD1, half, ny)
    shapes2 = (group + 2 * PAD2, half // 2, ny)
    direction, image, smooth2, weight, pay2, w1r, w1i, w2r, w2i = call(
        functools.partial(second_kernel, masks, layout),
        [
            fine,
            (2, 12, nx, ny),
            (2, 10, nx, ny),
            window,
            (2 * half + 8, ny),
            shapes1,
            shapes1,
            shapes2,
            shapes2,
        ],
        [at, own, near, swap, skip, far, *gathered1],
        [window] * 4
        + [(WINDOW, nx, ny), (2, nx, ny), (10, half, ny), window, (group, half // 2, ny)]
        + coarse_shapes(group, nx, ny),
        "second",
    )
    xtable, qrow = pl.pallas_call(
        functools.partial(phase_kernel, masks, layout, 4 * half),
        out_shape=[full((2 * nx, group * ny // 2)), full((8, group * ny // 2))],
        in_specs=[SM] + [VM] * len(gathered1),
        out_specs=[VM] * 2,
        scratch_shapes=[pltpu.VMEM((group, ny), F32)],
        cost_estimate=pl.CostEstimate(flops=4000000, bytes_accessed=600000, transcendentals=0),
        name="phases",
    )(at, *gathered1)
    gathered2, masks, layout = gather(pay2, group)
    corrected, last_image, halfway, pay3, alpha = call(
        functools.partial(third_kernel, masks, layout),
        [fine, fine, fine, (group, 8, ny), (8, ny)],
        [
            at,
            own,
            direction,
            image,
            smooth2,
            weight,
            w1r,
            w1i,
            w2r,
            w2i,
            jnp.asarray(y_phases(nx, ny)),
            xtable,
            qrow,
            *gathered2,
        ],
        [(2, 12, nx, ny), (2, 12, nx, ny), (2, nx, ny), (6, half, ny)] + coarse_shapes(group, nx, ny),
        "third",
    )
    got = lax.all_to_all(pay3, "gz", 0, 0)
    solution, residual, pupil = call(
        last_kernel,
        [fine, fine, (2, ny // 2)],
        [at, direction, corrected, last_image, halfway, alpha, got],
        [],
        "last",
    )
    return solution, residual, pupil


def solution(mesh):
    return jax.shard_map(
        on_device,
        mesh=mesh,
        in_specs=(
            P(None, ("clip", "gz"), None, None),
            P(("clip", "gz"), None, None),
            P(None, "gz"),
        ),
        out_specs=(
            P(None, ("clip", "gz"), None, None),
            P(None, ("clip", "gz"), None, None),
            P(None, ("clip", "gz")),
        ),
        check_vma=False,
    )
```

```python
import functools
import math

import jax
import jax.numpy as jnp
import numpy as np
from jax import lax
from jax.experimental import pallas as pl
from jax.experimental.pallas import tpu as pltpu
from jax.sharding import PartitionSpec as P


ORD_HALF = 22
HELM_TABLE = ((-0.5, 0.0), (1.0, -1.4), (-1.2, 0.0))
SHIFT_TABLE = ((-0.5, -0.25), (1.0, -0.25 * math.sqrt(11.84)), (-1.2, -0.6))
RELAX = 0.8
KEEP = 1.0 - RELAX
PLANES = 4
OWN = 2 * PLANES
WINDOW = 5 * PLANES
PAD1 = 8
PAD2 = 4
H1 = 0.25
H2 = 0.0625
F32 = jnp.float32
VMEM_LIMIT = 28 * 2**20

WEIGHTS = tuple(RELAX / complex(6.0 + s[0], s[1]) for s in SHIFT_TABLE)


def pick(code, values):
    return jnp.where(
        code == 1.0,
        values[0],
        jnp.where(code == 2.0, values[1], jnp.where(code == 3.0, values[2], 0.0)),
    )


def weight_of(code):
    return pick(code, [w.real for w in WEIGHTS]), pick(code, [w.imag for w in WEIGHTS])


def shift_of(code):
    return pick(code, [s[0] for s in SHIFT_TABLE]), pick(code, [s[1] for s in SHIFT_TABLE])


def helm_of(code):
    return pick(code, [s[0] for s in HELM_TABLE]), pick(code, [s[1] for s in HELM_TABLE])


def cmul(ar, ai, br, bi):
    return ar * br - ai * bi, ar * bi + ai * br


HALO = 8
CHUNK = 16


def put(ref, c, p, r0, value, nx):
    n = value.shape[0]
    ref[c, p, pl.ds(HALO + r0, n), :] = value
    if r0 == 0:
        ref[c, p, pl.ds(HALO + nx, 1), :] = value[:1]
    if r0 + n == nx:
        ref[c, p, pl.ds(HALO - 1, 1), :] = value[n - 1 :]


def mid(ref, c, p, r0, n=CHUNK):
    return ref[c, p, pl.ds(HALO + r0, n), :]


def around(ref, p, r0, zero):
    sums = []
    for c in range(2):
        m = mid(ref, c, p, r0)
        ny = m.shape[1]
        total = mid(ref, c, p - 1, r0) + mid(ref, c, p + 1, r0)
        total = total + ref[c, p, pl.ds(HALO - 1 + r0 + zero, CHUNK), :]
        total = total + ref[c, p, pl.ds(HALO + 1 + r0 + zero, CHUNK), :]
        total = total + pltpu.roll(m, 1, 1) + pltpu.roll(m, ny - 1, 1)
        sums.append(total)
    return sums


def planes_of(lower, upper, nx, body, most=4):
    size = max(n for n in range(1, most + 1) if (upper - lower) % n == 0)

    def step(k, carry):
        for j in range(size):
            for r0 in range(0, nx, CHUNK):
                body(lower + k * size + j, r0, pl.ds(r0, CHUNK))
        return carry

    lax.fori_loop(0, (upper - lower) // size, step, 0)


def lanes(shape):
    return lax.broadcasted_iota(jnp.int32, shape, len(shape) - 1)


def put_packed(ref, p, count, value):
    n = value.shape[1]
    ref[pl.ds(p, count), pl.ds(HALO, n), :] = value
    ref[pl.ds(p, count), pl.ds(HALO + n, 1), :] = value[:, :1]
    ref[pl.ds(p, count), pl.ds(HALO - 1, 1), :] = value[:, n - 1 :]


def mid_packed(ref, p, count):
    return ref[pl.ds(p, count), pl.ds(HALO, ref.shape[1] - 2 * HALO), :]


def around_packed(ref, p, count, part, zero):
    m = mid_packed(ref, p, count)
    n, width = m.shape[1:]
    total = mid_packed(ref, p - 1, count) + mid_packed(ref, p + 1, count)
    total = total + ref[pl.ds(p, count), pl.ds(HALO - 1 + zero, n), :]
    total = total + ref[pl.ds(p, count), pl.ds(HALO + 1 + zero, n), :]
    at = lanes((1, 1, width)) % part
    before = jnp.where(at == 0, pltpu.roll(m, width + 1 - part, 2), pltpu.roll(m, 1, 2))
    after = jnp.where(at == part - 1, pltpu.roll(m, part - 1, 2), pltpu.roll(m, width - 1, 2))
    return total + before + after


def cmul_packed(wr, wi, g, part):
    return wr * g + wi * pltpu.roll(g, part, g.ndim - 1)


def weights_packed(shift, part, factor):
    other = pltpu.roll(shift, part, 1)
    real_lane = lanes(shift.shape) % (2 * part) < part
    dr = 6.0 * factor + jnp.where(real_lane, shift, other)
    di = jnp.where(real_lane, other, shift)
    scale = RELAX / (dr * dr + di * di)
    return jnp.where(real_lane, dr, -di) * scale


def dot(a, b):
    return jnp.dot(a, b, precision=lax.Precision.HIGHEST, preferred_element_type=F32)


def iota2(rows, cols):
    return (
        lax.broadcasted_iota(jnp.int32, (rows, cols), 0),
        lax.broadcasted_iota(jnp.int32, (rows, cols), 1),
    )


def restrict_fine(tmp):
    nx, ny = tmp.shape[1:]
    half = nx // 2
    rows = [tmp[c, pl.ds(0, half, stride=2), :] + tmp[c, pl.ds(1, half, stride=2), :] for c in range(2)]
    r, c = iota2(2 * ny, ny)
    pool = jnp.where(r // 2 == c, 0.125, 0.0).astype(F32)
    return dot(jnp.concatenate(rows, axis=1), pool)


def pool_level1(ny):
    r, c = iota2(ny, ny)
    return jnp.where(r // 2 == c % (ny // 2), 0.125, 0.0).astype(F32)


def full(shape_dtype):
    return jax.ShapeDtypeStruct(shape_dtype, F32)


VM = pl.BlockSpec(memory_space=pltpu.VMEM)
SM = pl.BlockSpec(memory_space=pltpu.SMEM)


def call(body, outs, inputs, scratch):
    size = sum(4 * math.prod(x.shape) for x in inputs) + sum(4 * math.prod(o) for o in outs)
    return pl.pallas_call(
        body,
        out_shape=[full(o) for o in outs],
        in_specs=[SM] + [VM] * (len(inputs) - 1),
        out_specs=[VM] * len(outs),
        scratch_shapes=[pltpu.VMEM(s, F32) for s in scratch],
        compiler_params=pltpu.CompilerParams(vmem_limit_bytes=VMEM_LIMIT),
        cost_estimate=pl.CostEstimate(flops=40 * size, bytes_accessed=size, transcendentals=0),
    )(*inputs)


def first_kernel(at, own, near, swap, orders, out, u, e1, u2, tmp, tmp1):
    odd, zero = at[1], at[2]
    nx, ny = own.shape[2:]

    def fill(block, lower, upper, first):
        def body(p, r0, rows):
            wr, wi = weight_of(block[2, p, rows])
            ur, ui = cmul(wr, wi, block[0, p, rows], block[1, p, rows])
            put(u, 0, first + p, r0, ur, nx)
            put(u, 1, first + p, r0, ui, nx)

        planes_of(lower, upper, nx, body)

    fill(own, 0, PLANES, 2)

    @pl.when(odd == 0)
    def _():
        fill(swap, 2, 4, -2)
        fill(near, 0, 2, 6)

    @pl.when(odd == 1)
    def _():
        fill(near, 2, 4, -2)
        fill(swap, 0, 2, 6)

    def smooth(p, block, q, r0, rows):
        sr, si = around(u, p, r0, zero)
        er = KEEP * block[0, q, rows] + sr
        ei = KEEP * block[1, q, rows] + si
        wr, wi = weight_of(block[2, q, rows])
        vr, vi = cmul(wr, wi, er, ei)
        put(u2, 0, p, r0, vr, nx)
        put(u2, 1, p, r0, vi, nx)
        return er, ei

    def inner(q, r0, rows):
        er, ei = smooth(2 + q, own, q, r0, rows)
        e1[0, q, rows] = er
        e1[1, q, rows] = ei

    planes_of(0, PLANES, nx, inner)

    def outer(block, q, p):
        planes_of(q, q + 1, nx, lambda q, r0, rows: smooth(p, block, q, r0, rows))

    @pl.when(odd == 0)
    def _():
        outer(swap, PLANES - 1, 1)
        outer(near, 0, 6)

    @pl.when(odd == 1)
    def _():
        outer(near, PLANES - 1, 1)
        outer(swap, 0, 6)

    half = nx // 2
    planes = []
    for q in range(PLANES // 2):
        for r0 in range(0, nx, CHUNK):
            rows = pl.ds(r0, CHUNK)
            total = [0.0, 0.0, 0.0, 0.0]
            for p in (2 * q, 2 * q + 1):
                s = around(u2, 2 + p, r0, zero)
                shift = shift_of(own[2, p, rows])
                for c in range(2):
                    total[c] = total[c] + KEEP * e1[c, p, rows] + s[c]
                    total[2 + c] = total[2 + c] + shift[c]
            for k in range(4):
                tmp[q, k // 2, k % 2, rows] = total[k]
        out[pl.ds(half * q, half), :] = restrict_fine(tmp.at[q, 0])
        shift = restrict_fine(tmp.at[q, 1])
        out[pl.ds(half * (2 + q), half), :] = weights_packed(shift, ny // 2, H1)
        planes.append(shift)
    tmp1[...] = planes[0] + planes[1]
    pooled = tmp1[pl.ds(0, half // 2, stride=2), :] + tmp1[pl.ds(1, half // 2, stride=2), :]
    shift2 = dot(pooled, pool_level1(ny))
    out[pl.ds(4 * half, half // 2), :] = weights_packed(shift2, ny // 4, H2)
    out[pl.ds(4 * half + half // 2, 8), :] = jnp.broadcast_to(orders[...], (8, ny))


def coarse_shapes(group, nx, ny):
    n1 = (2 * group + 2 * PAD1, nx // 2 + 2 * HALO, ny)
    n2 = (group + 2 * PAD2, nx // 4 + 2 * HALO, ny)
    return [n1[:1] + (nx // 2, ny), n1, n1, n1, n1, n2[:1] + (nx // 4, ny), n2, n2, (nx // 2, ny), (group * (nx // 2), ny)]


def clear_edges(ref, pad, count):
    zero = jnp.zeros(ref.shape[1:], F32)
    top = ref.shape[0] - pad
    for k in range(count):
        ref[pad - 1 - k] = zero
        ref[top + k] = zero


def coarse_weights(me, masks, pieces, w1r, w1i, w2r, w2i):
    half, ny = w1r.shape[1:]
    quarter = half // 2
    for ref, pad in ((w1r, PAD1), (w1i, PAD1), (w2r, PAD2), (w2i, PAD2)):
        clear_edges(ref, pad, pad - 1)

    def expand(w, part):
        other = pltpu.roll(w, part, 1)
        real_lane = lanes(w.shape) % (2 * part) < part
        return jnp.where(real_lane, w, other), jnp.where(real_lane, -other, w)

    for mask, (piece, j) in zip(masks, pieces, strict=True):
        d = me ^ mask
        for k in range(2):
            wr, wi = expand(piece[j, pl.ds(half * (2 + k), half), :], ny // 2)
            w1r[PAD1 + 2 * d + k] = wr
            w1i[PAD1 + 2 * d + k] = wi
        wr, wi = expand(piece[j, pl.ds(4 * half, quarter), :], ny // 4)
        w2r[PAD2 + d] = wr
        w2i[PAD2 + d] = wi


def chunked(lower, count, most, body):
    size = max(n for n in range(1, most + 1) if count % n == 0)

    def step(k, carry):
        body(lower + k * size, size)
        return carry

    lax.fori_loop(0, count // size, step, 0)


def coarse_solve(me, zero, masks, pieces, reach, w1r, w1i, w2r, w2i, g1, u1, u2, v1, e1, g2, va, vb, tmp, pool, out):
    half, ny = tmp.shape
    quarter = half // 2
    group = len(masks)
    part1, part2 = ny // 2, ny // 4
    n1 = 2 * group
    clear_edges(g1, PAD1, PAD1 - 1)
    clear_edges(u1, PAD1, 1)
    clear_edges(u2, PAD1, 1)
    clear_edges(v1, PAD1, PAD1 - 1)
    clear_edges(va, PAD2, 1)
    clear_edges(vb, PAD2, PAD2 - 1)
    for mask, (piece, j) in zip(masks, pieces, strict=True):
        p = PAD1 + 2 * (me ^ mask)
        g = piece[j, pl.ds(0, 2 * half), :].reshape(2, half, ny)
        g1[pl.ds(p, 2)] = g
        put_packed(u1, p, 2, cmul_packed(w1r[pl.ds(p, 2)], w1i[pl.ds(p, 2)], g, part1))

    def pre(p, n):
        e = KEEP * g1[pl.ds(p, n)] + H1 * around_packed(u1, p, n, part1, zero)
        u = cmul_packed(w1r[pl.ds(p, n)], w1i[pl.ds(p, n)], e, part1)
        e1[pl.ds(p, n), pl.ds(0, half), :] = e
        put_packed(u2, p, n, u)
        put_packed(v1, p, n, mid_packed(u1, p, n) + u)

    chunked(PAD1, n1, 8, pre)

    def coarser(p, n):
        e = KEEP * e1[pl.ds(p, n), pl.ds(0, half), :] + H1 * around_packed(u2, p, n, part1, zero)
        e = e.reshape(n // 2, 2, half, ny)
        pairs = (e[:, 0] + e[:, 1]).reshape(n // 2 * half, ny)
        pool[pl.ds((p - PAD1) // 2 * half, n // 2 * half), :] = pairs

    chunked(PAD1, n1, 8, coarser)
    rows = group * quarter
    flat = pool[pl.ds(0, rows, stride=2), :] + pool[pl.ds(1, rows, stride=2), :]
    r2 = dot(flat, pool_level1(ny)).reshape(group, quarter, ny)
    inside = pl.ds(PAD2, group)
    g2[inside] = r2
    put_packed(va, PAD2, group, cmul_packed(w2r[inside], w2i[inside], r2, part2))
    for src, dst in ((va, vb), (vb, va), (va, vb)):

        def sweep(p, n, src=src, dst=dst):
            s = g2[pl.ds(p, n)] + H2 * around_packed(src, p, n, part2, zero)
            v = KEEP * mid_packed(src, p, n) + cmul_packed(w2r[pl.ds(p, n)], w2i[pl.ds(p, n)], s, part2)
            put_packed(dst, p, n, v)

        chunked(PAD2, group, 16, sweep)
    reach2 = (reach + 2) // 2
    count = 2 * reach2 + 1
    flat = mid_packed(vb, PAD2 + me - reach2, count).reshape(count * quarter, ny)
    r, c = iota2(ny, ny)
    spread = jnp.where(c // 2 == r, 1.0, 0.0).astype(F32)
    e2 = dot(flat, spread)
    pool[pl.ds(0, count * quarter, stride=2), :] = e2
    pool[pl.ds(1, count * quarter, stride=2), :] = e2
    base = PAD1 + 2 * (me - reach2)
    for k in range(count):
        add = pool[pl.ds(k * half, half), :]
        both = mid_packed(v1, base + 2 * k, 2) + add[None]
        put_packed(v1, base + 2 * k, 2, both)

    def post(src, p, n):
        s = g1[pl.ds(p, n)] + H1 * around_packed(src, p, n, part1, zero)
        return KEEP * mid_packed(src, p, n) + cmul_packed(w1r[pl.ds(p, n)], w1i[pl.ds(p, n)], s, part1)

    start = PAD1 + 2 * me

    def third(p, n):
        put_packed(u1, p, n, post(v1, p, n))

    def fourth(p, n):
        out[pl.ds(p - (start - reach), n)] = post(u1, p, n)

    chunked(start - reach - 1, 2 * reach + 4, 6, third)
    chunked(start - reach, 2 * reach + 2, 5, fourth)


def add_correction(ec, v, tmp, planes, nx):
    half, ny = ec.shape[1:]
    r, c = iota2(ny, 2 * ny)
    spread = jnp.where(c // 2 == r, 1.0, 0.0).astype(F32)

    def body(m, carry):
        k = 2 * m
        both = dot(ec[pl.ds(k, 2)].reshape(2 * half, ny), spread)
        for j in range(2):
            for c in range(2):
                e = both[j * half : (j + 1) * half, c * ny : (c + 1) * ny]
                tmp[j, c, pl.ds(0, half, stride=2), :] = e
                tmp[j, c, pl.ds(1, half, stride=2), :] = e
        for j in range(2):
            for c in range(2):
                for r0 in range(0, nx, CHUNK):
                    add = tmp[j, c, pl.ds(r0, CHUNK)]
                    for p in (2 * (k + j), 2 * (k + j) + 1):
                        put(v, c, p, r0, mid(v, c, p, r0) + add, nx)
        return carry

    lax.fori_loop(0, planes // 2, body, 0)


def second_kernel(masks, layout, at, own, near, swap, skip, far, *refs):
    n = max(i for i, _ in layout) + 1
    gathered, refs = refs[:n], refs[n:]
    (direction, image, smooth2, weight8, pay, w1r, w1i, w2r, w2i), refs = refs[:9], refs[9:]
    f, weight, u, u2, v, code, tmp, ec, e1 = refs[:9]
    coarse = refs[9:]
    me, odd, zero = at[0], at[1], at[2]
    nx, ny = own.shape[2:]
    pieces = [(gathered[i], j) for i, j in layout]

    def fill(block, first):
        def body(q, r0, rows):
            p = first + q
            c = block[2, q, rows]
            wr, wi = weight_of(c)
            fr, fi = block[0, q, rows], block[1, q, rows]
            ur, ui = cmul(wr, wi, fr, fi)
            f[0, p, rows], f[1, p, rows] = fr, fi
            weight[0, p, rows], weight[1, p, rows] = wr, wi
            put(u, 0, p, r0, ur, nx)
            put(u, 1, p, r0, ui, nx)
            code[p, rows] = c

        planes_of(0, PLANES, nx, body)

    fill(own, OWN)
    fill(near, OWN + PLANES - 2 * PLANES * odd)
    fill(swap, OWN - PLANES + 2 * PLANES * odd)
    fill(skip, 4 * PLANES * odd)
    fill(far, 4 * PLANES - 4 * PLANES * odd)

    def pre(p, r0, rows):
        sr, si = around(u, p, r0, zero)
        er = KEEP * f[0, p, rows] + sr
        ei = KEEP * f[1, p, rows] + si
        vr, vi = cmul(weight[0, p, rows], weight[1, p, rows], er, ei)
        put(v, 0, p, r0, mid(u, 0, p, r0) + vr, nx)
        put(v, 1, p, r0, mid(u, 1, p, r0) + vi, nx)

    planes_of(1, WINDOW - 1, nx, pre, 6)
    coarse_weights(me, masks, pieces, w1r, w1i, w2r, w2i)
    coarse_solve(me, zero, masks, pieces, 4, w1r, w1i, w2r, w2i, *coarse, ec)
    add_correction(ec, v, tmp, WINDOW // 2, nx)

    def sweep(src, dst, p, r0, rows):
        sr, si = around(src, p, r0, zero)
        vr, vi = cmul(weight[0, p, rows], weight[1, p, rows], f[0, p, rows] + sr, f[1, p, rows] + si)
        put(dst, 0, p, r0, KEEP * mid(src, 0, p, r0) + vr, nx)
        put(dst, 1, p, r0, KEEP * mid(src, 1, p, r0) + vi, nx)

    planes_of(2, WINDOW - 2, nx, lambda *a: sweep(v, u, *a))
    planes_of(3, WINDOW - 3, nx, lambda *a: sweep(u, v, *a), 7)

    def apply(p, r0, rows):
        sr, si = around(v, p, r0, zero)
        c = code[p, rows]
        hr, hi = helm_of(c)
        vr, vi = mid(v, 0, p, r0), mid(v, 1, p, r0)
        ar, ai = cmul(hr, hi, vr, vi)
        ar = jnp.where(c > 0.0, ar + 6.0 * vr - sr, 0.0)
        ai = jnp.where(c > 0.0, ai + 6.0 * vi - si, 0.0)
        image[0, p - 4, rows] = ar
        image[1, p - 4, rows] = ai
        ur, ui = cmul(weight[0, p, rows], weight[1, p, rows], ar, ai)
        put(u, 0, p, r0, ur, nx)
        put(u, 1, p, r0, ui, nx)

    planes_of(4, WINDOW - 4, nx, apply)
    rho, cross_r, cross_i = 0.0, 0.0, 0.0
    for q in range(PLANES):
        for r0 in range(0, nx, CHUNK):
            rows = pl.ds(r0, CHUNK)
            fr, fi = own[0, q, rows], own[1, q, rows]
            ir, ii = image[0, OWN - 4 + q, rows], image[1, OWN - 4 + q, rows]
            rho = rho + fr * fr + fi * fi
            cross_r = cross_r + fr * ir + fi * ii
            cross_i = cross_i + fr * ii - fi * ir
            for c in range(2):
                direction[c, q, rows] = mid(v, c, OWN + q, r0)
    half = nx // 2
    row = lax.broadcasted_iota(jnp.int32, (8, ny), 0)
    sums = [jnp.sum(t, axis=0, keepdims=True) for t in (rho, cross_r, cross_i)]
    tail = jnp.where(row == 0, sums[0], jnp.where(row == 1, sums[1], jnp.where(row == 2, sums[2], 0.0)))
    pay[pl.ds(2 * half, 8), :] = tail

    def pre2(p, r0, rows):
        sr, si = around(u, p, r0, zero)
        er = KEEP * image[0, p - 4, rows] + sr
        ei = KEEP * image[1, p - 4, rows] + si
        vr, vi = cmul(weight[0, p, rows], weight[1, p, rows], er, ei)
        e1[0, p, rows], e1[1, p, rows] = er, ei
        put(u2, 0, p, r0, vr, nx)
        put(u2, 1, p, r0, vi, nx)
        smooth2[0, p - 5, rows] = mid(u, 0, p, r0) + vr
        smooth2[1, p - 5, rows] = mid(u, 1, p, r0) + vi

    planes_of(5, WINDOW - 5, nx, pre2, 5)
    for q in range(PLANES // 2):
        for r0 in range(0, nx, CHUNK):
            rows = pl.ds(r0, CHUNK)
            total = [0.0, 0.0]
            for k in range(2):
                p = OWN + 2 * q + k
                s = around(u2, p, r0, zero)
                for c in range(2):
                    total[c] = total[c] + KEEP * e1[c, p, rows] + s[c]
            for c in range(2):
                tmp[q, c, rows] = total[c]
        pay[pl.ds(half * q, half), :] = restrict_fine(tmp.at[q])

    def copy(p, r0, rows):
        for c in range(2):
            weight8[c, p, rows] = weight[c, p + OWN - 2, rows]

    planes_of(0, PLANES + 4, nx, copy)


def phase_kernel(masks, layout, row, at, *refs):
    n = max(i for i, _ in layout) + 1
    gathered = refs[:n]
    table, qrow, found = refs[n:]
    me = at[0]
    ny = found.shape[1]
    nx = table.shape[0] // 2
    for mask, (i, j) in zip(masks, layout, strict=True):
        found[pl.ds(me ^ mask, 1), :] = gathered[i][j, pl.ds(row, 1), :]
    low = lanes((1, ny)) < ny // 2
    x = lax.broadcasted_iota(jnp.int32, (nx, ny), 0)
    for pair in range(len(masks) // 2):
        even = found[pl.ds(2 * pair, 1), :]
        odd = found[pl.ds(2 * pair + 1, 1), :]
        p = jnp.where(low, even, pltpu.roll(odd, ny // 2, 1))
        q = jnp.where(low, pltpu.roll(even, ny // 2, 1), odd)
        turns = (x * p.astype(jnp.int32)) & (nx - 1)
        angle = turns.astype(F32) * (2.0 * math.pi / nx)
        table[pl.ds(0, nx), pl.ds(pair * ny, ny)] = jnp.cos(angle)
        table[pl.ds(nx, nx), pl.ds(pair * ny, ny)] = -jnp.sin(angle)
        qrow[:, pl.ds(pair * ny, ny)] = jnp.broadcast_to(q, (8, ny))


def third_kernel(
    masks, layout, at, own, direction, image, smooth2, weight8, w1r, w1i, w2r, w2i, ytable, xtable, qrow, *refs
):
    n = max(i for i, _ in layout) + 1
    gathered, refs = refs[:n], refs[n:]
    (corrected, last_image, halfway, pay, alpha), refs = refs[:5], refs[5:]
    u, v, tmp, ec = refs[:4]
    coarse = refs[4:]
    me, zero = at[0], at[2]
    pieces = [(gathered[i], j) for i, j in layout]
    nx, ny = own.shape[2:]
    half = nx // 2
    coarse_solve(me, zero, masks, pieces, 2, w1r, w1i, w2r, w2i, *coarse, ec)

    def take(p, r0, rows):
        for c in range(2):
            put(v, c, p, r0, smooth2[c, p - 1, rows], nx)

    planes_of(1, 11, nx, take)
    add_correction(ec, v, tmp, 6, nx)

    def sweep(src, dst, p, r0, rows):
        sr, si = around(src, p, r0, zero)
        wr, wi = weight8[0, p - 2, rows], weight8[1, p - 2, rows]
        vr, vi = cmul(wr, wi, image[0, p, rows] + sr, image[1, p, rows] + si)
        put(dst, 0, p, r0, KEEP * mid(src, 0, p, r0) + vr, nx)
        put(dst, 1, p, r0, KEEP * mid(src, 1, p, r0) + vi, nx)

    planes_of(2, 10, nx, lambda *a: sweep(v, u, *a))
    planes_of(3, 9, nx, lambda *a: sweep(u, v, *a))

    sums = 0.0
    for i, j in layout:
        sums = sums + gathered[i][j, pl.ds(2 * half, 8), :]
    rho, cr, ci = [jnp.sum(sums[k : k + 1], axis=1, keepdims=True) for k in range(3)]
    modulus = cr * cr + ci * ci
    ar = rho * cr / modulus
    ai = -rho * ci / modulus
    dots = [0.0, 0.0, 0.0]
    for q in range(PLANES):
        for r0 in range(0, nx, CHUNK):
            rows = pl.ds(r0, CHUNK)
            p = 4 + q
            sr, si = around(v, p, r0, zero)
            hr, hi = helm_of(own[2, q, rows])
            wr, wi = mid(v, 0, p, r0), mid(v, 1, p, r0)
            br, bi = cmul(hr, hi, wr, wi)
            br, bi = br + 6.0 * wr - sr, bi + 6.0 * wi - si
            ir, ii = image[0, p, rows], image[1, p, rows]
            br, bi = cmul(ar, ai, br, bi)
            lr, li = ir - br, ii - bi
            tr, ti = cmul(ar, ai, ir, ii)
            hr, hi = own[0, q, rows] - tr, own[1, q, rows] - ti
            xr, xi = cmul(ar, ai, wr, wi)
            corrected[0, q, rows], corrected[1, q, rows] = direction[0, q, rows] - xr, direction[1, q, rows] - xi
            last_image[0, q, rows], last_image[1, q, rows] = lr, li
            halfway[0, q, rows], halfway[1, q, rows] = hr, hi
            dots[0] = dots[0] + lr * hr + li * hi
            dots[1] = dots[1] + lr * hi - li * hr
            dots[2] = dots[2] + lr * lr + li * li
    dots = [jnp.sum(t, axis=0, keepdims=True) for t in dots]
    row = lax.broadcasted_iota(jnp.int32, (8, ny), 0)
    alpha[...] = jnp.where(row == 0, ar, ai)

    sign = jnp.where(lanes((nx, ny)) < ny // 2, -1.0, 1.0)
    stacked = []
    for field in (direction, corrected):
        plane = field[:, PLANES - 1].reshape(2 * nx, ny)
        m = lax.dot_general(
            ytable[...],
            plane,
            (((1,), (1,)), ((), ())),
            precision=lax.Precision.HIGHEST,
            preferred_element_type=F32,
        )
        t = m[:nx] + sign * pltpu.roll(m[nx:], nx, 1)
        stacked += [-sign * t, pltpu.roll(t, nx, 1)]
    spectrum = dot(jnp.concatenate(stacked, axis=0), xtable[...])
    scale = 1.0 / math.sqrt(nx * ny)
    at_row = lax.broadcasted_iota(jnp.int32, (nx, ny), 0).astype(F32) - ORD_HALF
    for pair in range(len(masks) // 2):
        chosen = at_row == qrow[0:1, pair * ny : (pair + 1) * ny]
        found = [
            scale
            * jnp.sum(
                jnp.where(chosen, spectrum[k * nx : (k + 1) * nx, pair * ny : (pair + 1) * ny], 0.0),
                axis=0,
                keepdims=True,
            )
            for k in range(4)
        ]
        block = 0.0
        for k, line in enumerate(found + dots):
            block = jnp.where(row == k, line, block)
        pay[2 * pair] = block
        pay[2 * pair + 1] = block


def last_kernel(at, direction, corrected, last_image, halfway, alpha, got, solution, residual, pupil):
    group = got.shape[0]
    nx, ny = direction.shape[2:]
    total = got[0]
    for k in range(1, group):
        total = total + got[k]
    along_r, along_i, norm = [jnp.sum(total[k : k + 1], axis=1, keepdims=True) for k in (4, 5, 6)]
    wr = along_r / norm
    wi = along_i / norm
    ar = alpha[0:1, 0:1]
    ai = alpha[1:2, 0:1]
    for q in range(PLANES):
        for r0 in range(0, nx, CHUNK):
            rows = pl.ds(r0, CHUNK)
            xr, xi = cmul(ar, ai, direction[0, q, rows], direction[1, q, rows])
            yr, yi = cmul(wr, wi, corrected[0, q, rows], corrected[1, q, rows])
            solution[0, q, rows], solution[1, q, rows] = xr + yr, xi + yi
            zr, zi = cmul(wr, wi, last_image[0, q, rows], last_image[1, q, rows])
            residual[0, q, rows], residual[1, q, rows] = halfway[0, q, rows] - zr, halfway[1, q, rows] - zi
    tip = got[group - 1]
    xr, xi = cmul(ar, ai, tip[0:1], tip[1:2])
    yr, yi = cmul(wr, wi, tip[2:3], tip[3:4])
    both = jnp.concatenate([xr + yr, xi + yi] * 4, axis=0)
    both = jnp.where(at[1] == 1, pltpu.roll(both, ny // 2, 1), both)
    pupil[...] = both[:2, : ny // 2]


def exchange(x, mask, group):
    return lax.ppermute(x, "gz", [(i, i ^ mask) for i in range(group)])


def swap_across(x, group):
    pairs = []
    for i in range(1, group - 1, 2):
        pairs += [(i, i + 1), (i + 1, i)]
    return lax.ppermute(x, "gz", pairs)


def skip_across(x, group):
    pairs = []
    for i in range(group):
        target = i + 2 if i % 2 == 0 else i - 2
        if 0 <= target < group:
            pairs.append((i, target))
    return lax.ppermute(x, "gz", pairs)


def stages_of(group):
    stages = [[1]]
    stride = 2
    left = group // 2
    if left.bit_length() % 2 == 0:
        stages.insert(0, [stride])
        stride, left = 2 * stride, left // 2
    while left > 1:
        stages.insert(0, [stride, 2 * stride, 3 * stride])
        stride, left = 4 * stride, left // 4
    return stages


def gather(x, group):
    have, masks = x[None], [0]
    stages = stages_of(group)
    for masks_now in stages[:-1]:
        got = [exchange(have, m, group) for m in masks_now]
        masks = masks + [k ^ m for m in masks_now for k in masks]
        have = jnp.concatenate([have] + got, axis=0)
    (m,) = stages[-1]
    other = exchange(have, m, group)
    count = len(masks)
    layout = [(0, j) for j in range(count)] + [(1, j) for j in range(count)]
    return [have, other], masks + [k ^ m for k in masks], layout


def y_phases(nx, ny):
    q = np.arange(nx) - ORD_HALF
    turns = (q[:, None] * np.arange(ny)[None, :]) % ny
    angle = turns.astype(np.float64) * (2.0 * np.pi / ny)
    return np.concatenate([np.cos(angle), -np.sin(angle)], axis=0).astype(np.float32)


def on_device(source_term, material, orders):
    group = lax.axis_size("gz")
    _, planes, nx, ny = source_term.shape
    assert planes == PLANES and 2 * nx == ny and 2 * orders.shape[1] == ny
    me = lax.axis_index("gz")
    at = jnp.stack([me, me % 2, me * 0]).astype(jnp.int32)
    half = nx // 2

    own = jnp.concatenate([source_term, (material + 1).astype(F32)[None]], axis=0)
    near = exchange(own, 1, group)
    swap = swap_across(own, group)
    order_row = orders.astype(F32).reshape(1, ny)
    fine = (2, PLANES, nx, ny)
    tall = nx + 2 * HALO
    (pay1,) = call(
        first_kernel,
        [(4 * half + half // 2 + 8, ny)],
        [at, own, near, swap, order_row],
        [(2, 8, tall, ny), fine, (2, 8, tall, ny), (2, 2, 2, nx, ny), (half, ny)],
    )
    gathered1, masks, layout = gather(pay1, group)
    skip = skip_across(own, group)
    far = exchange(swap, 1, group)

    window = (2, WINDOW, nx, ny)
    haloed = (2, WINDOW, tall, ny)
    shapes1 = (2 * group + 2 * PAD1, half, ny)
    shapes2 = (group + 2 * PAD2, half // 2, ny)
    direction, image, smooth2, weight8, pay2, w1r, w1i, w2r, w2i = call(
        functools.partial(second_kernel, masks, layout),
        [
            fine,
            (2, 12, nx, ny),
            (2, 10, nx, ny),
            (2, PLANES + 4, nx, ny),
            (2 * half + 8, ny),
            shapes1,
            shapes1,
            shapes2,
            shapes2,
        ],
        [at, own, near, swap, skip, far, *gathered1],
        [window, window, haloed, haloed, haloed, (WINDOW, nx, ny), (2, 2, nx, ny), (10, half, ny), window]
        + coarse_shapes(group, nx, ny),
    )
    xtable, qrow = call(
        functools.partial(phase_kernel, masks, layout, 4 * half + half // 2),
        [(2 * nx, group * ny // 2), (8, group * ny // 2)],
        [at, *gathered1],
        [(group, ny)],
    )
    gathered2, masks, layout = gather(pay2, group)
    corrected, last_image, halfway, pay3, alpha = call(
        functools.partial(third_kernel, masks, layout),
        [fine, fine, fine, (group, 8, ny), (8, ny)],
        [
            at,
            own,
            direction,
            image,
            smooth2,
            weight8,
            w1r,
            w1i,
            w2r,
            w2i,
            jnp.asarray(y_phases(nx, ny)),
            xtable,
            qrow,
            *gathered2,
        ],
        [(2, 12, tall, ny), (2, 12, tall, ny), (2, 2, nx, ny), (6, half, ny)] + coarse_shapes(group, nx, ny),
    )
    got = lax.all_to_all(pay3, "gz", 0, 0)
    solution, residual, pupil = call(
        last_kernel, [fine, fine, (2, ny // 2)], [at, direction, corrected, last_image, halfway, alpha, got], []
    )
    return solution, residual, pupil


def solution(mesh):
    return jax.shard_map(
        on_device,
        mesh=mesh,
        in_specs=(
            P(None, ("clip", "gz"), None, None),
            P(("clip", "gz"), None, None),
            P(None, "gz"),
        ),
        out_specs=(
            P(None, ("clip", "gz"), None, None),
            P(None, ("clip", "gz"), None, None),
            P(None, ("clip", "gz")),
        ),
        check_vma=False,
    )
```

```python
import functools
import math

import jax
import jax.numpy as jnp
import numpy as np
from jax import lax
from jax.experimental import pallas as pl
from jax.experimental.pallas import tpu as pltpu
from jax.sharding import PartitionSpec as P


ORD_HALF = 22
HELM_TABLE = ((-0.5, 0.0), (1.0, -1.4), (-1.2, 0.0))
SHIFT_TABLE = ((-0.5, -0.25), (1.0, -0.25 * math.sqrt(11.84)), (-1.2, -0.6))
RELAX = 0.8
KEEP = 1.0 - RELAX
PLANES = 4
OUTER = 2
OWN = PLANES + OUTER
WINDOW = PLANES + 2 * OWN
PAD1 = 8
PAD2 = 4
H1 = 0.25
H2 = 0.0625
F32 = jnp.float32
VMEM_LIMIT = 28 * 2**20

WEIGHTS = tuple(RELAX / complex(6.0 + s[0], s[1]) for s in SHIFT_TABLE)


def pick(code, values):
    return jnp.where(
        code == 1.0,
        values[0],
        jnp.where(code == 2.0, values[1], jnp.where(code == 3.0, values[2], 0.0)),
    )


def weight_of(code):
    return pick(code, [w.real for w in WEIGHTS]), pick(code, [w.imag for w in WEIGHTS])


def shift_of(code):
    return pick(code, [s[0] for s in SHIFT_TABLE]), pick(code, [s[1] for s in SHIFT_TABLE])


def helm_of(code):
    return pick(code, [s[0] for s in HELM_TABLE]), pick(code, [s[1] for s in HELM_TABLE])


def cmul(ar, ai, br, bi):
    return ar * br - ai * bi, ar * bi + ai * br


HALO = 8
CHUNK = 16


def put(ref, c, p, r0, value, nx):
    n = value.shape[0]
    ref[c, p, pl.ds(HALO + r0, n), :] = value
    if r0 == 0:
        ref[c, p, pl.ds(HALO + nx, 1), :] = value[:1]
    if r0 + n == nx:
        ref[c, p, pl.ds(HALO - 1, 1), :] = value[n - 1 :]


def mid(ref, c, p, r0, n=CHUNK):
    return ref[c, p, pl.ds(HALO + r0, n), :]


def around(ref, p, r0, zero):
    sums = []
    for c in range(2):
        m = mid(ref, c, p, r0)
        ny = m.shape[1]
        total = mid(ref, c, p - 1, r0) + mid(ref, c, p + 1, r0)
        total = total + ref[c, p, pl.ds(HALO - 1 + r0 + zero, CHUNK), :]
        total = total + ref[c, p, pl.ds(HALO + 1 + r0 + zero, CHUNK), :]
        total = total + pltpu.roll(m, 1, 1) + pltpu.roll(m, ny - 1, 1)
        sums.append(total)
    return sums


def planes_of(lower, upper, nx, body, most=4):
    size = max(n for n in range(1, most + 1) if (upper - lower) % n == 0)

    def step(k, carry):
        for j in range(size):
            for r0 in range(0, nx, CHUNK):
                body(lower + k * size + j, r0, pl.ds(r0, CHUNK))
        return carry

    lax.fori_loop(0, (upper - lower) // size, step, 0)


def lanes(shape):
    return lax.broadcasted_iota(jnp.int32, shape, len(shape) - 1)


def put_packed(ref, p, count, value):
    n = value.shape[1]
    ref[pl.ds(p, count), pl.ds(HALO, n), :] = value
    ref[pl.ds(p, count), pl.ds(HALO + n, 1), :] = value[:, :1]
    ref[pl.ds(p, count), pl.ds(HALO - 1, 1), :] = value[:, n - 1 :]


def mid_packed(ref, p, count):
    return ref[pl.ds(p, count), pl.ds(HALO, ref.shape[1] - 2 * HALO), :]


def around_packed(ref, p, count, part, zero):
    m = mid_packed(ref, p, count)
    n, width = m.shape[1:]
    total = mid_packed(ref, p - 1, count) + mid_packed(ref, p + 1, count)
    total = total + ref[pl.ds(p, count), pl.ds(HALO - 1 + zero, n), :]
    total = total + ref[pl.ds(p, count), pl.ds(HALO + 1 + zero, n), :]
    at = lanes((1, 1, width)) % part
    before = jnp.where(at == 0, pltpu.roll(m, width + 1 - part, 2), pltpu.roll(m, 1, 2))
    after = jnp.where(at == part - 1, pltpu.roll(m, part - 1, 2), pltpu.roll(m, width - 1, 2))
    return total + before + after


def cmul_packed(wr, wi, g, part):
    return wr * g + wi * pltpu.roll(g, part, g.ndim - 1)


def weights_packed(shift, part, factor):
    other = pltpu.roll(shift, part, 1)
    real_lane = lanes(shift.shape) % (2 * part) < part
    dr = 6.0 * factor + jnp.where(real_lane, shift, other)
    di = jnp.where(real_lane, other, shift)
    scale = RELAX / (dr * dr + di * di)
    return jnp.where(real_lane, dr, -di) * scale


def dot(a, b):
    return jnp.dot(a, b, precision=lax.Precision.HIGHEST, preferred_element_type=F32)


def iota2(rows, cols):
    return (
        lax.broadcasted_iota(jnp.int32, (rows, cols), 0),
        lax.broadcasted_iota(jnp.int32, (rows, cols), 1),
    )


def restrict_fine(tmp):
    nx, ny = tmp.shape[1:]
    half = nx // 2
    rows = [tmp[c, pl.ds(0, half, stride=2), :] + tmp[c, pl.ds(1, half, stride=2), :] for c in range(2)]
    r, c = iota2(2 * ny, ny)
    pool = jnp.where(r // 2 == c, 0.125, 0.0).astype(F32)
    return dot(jnp.concatenate(rows, axis=1), pool)


def pool_level1(ny):
    r, c = iota2(ny, ny)
    return jnp.where(r // 2 == c % (ny // 2), 0.125, 0.0).astype(F32)


def full(shape_dtype):
    return jax.ShapeDtypeStruct(shape_dtype, F32)


VM = pl.BlockSpec(memory_space=pltpu.VMEM)
SM = pl.BlockSpec(memory_space=pltpu.SMEM)


def call(body, outs, inputs, scratch):
    size = sum(4 * math.prod(x.shape) for x in inputs) + sum(4 * math.prod(o) for o in outs)
    return pl.pallas_call(
        body,
        out_shape=[full(o) for o in outs],
        in_specs=[SM] + [VM] * (len(inputs) - 1),
        out_specs=[VM] * len(outs),
        scratch_shapes=[pltpu.VMEM(s, F32) for s in scratch],
        compiler_params=pltpu.CompilerParams(vmem_limit_bytes=VMEM_LIMIT),
        cost_estimate=pl.CostEstimate(flops=40 * size, bytes_accessed=size, transcendentals=0),
    )(*inputs)


def pack_kernel(at, source, material, own, inner, outer):
    odd = at[1]
    nx = source.shape[2]

    def join(p, r0, rows):
        for c in range(2):
            own[c, p, rows] = source[c, p, rows]
        own[2, p, rows] = (material[p, rows] + 1).astype(F32)

    planes_of(0, PLANES, nx, join)

    def halves(p, r0, rows):
        for c in range(3):
            inner[c, p, rows] = own[c, p + OUTER * odd, rows]
            outer[c, p, rows] = own[c, p + OUTER * (1 - odd), rows]

    planes_of(0, OUTER, nx, halves)


def first_kernel(at, own, near, swap, static, out, u, e1, u2, tmp):
    odd, zero = at[1], at[2]
    nx, _ = own.shape[2:]

    def fill(block, lower, upper, first):
        def body(p, r0, rows):
            wr, wi = weight_of(block[2, p, rows])
            ur, ui = cmul(wr, wi, block[0, p, rows], block[1, p, rows])
            put(u, 0, first + p, r0, ur, nx)
            put(u, 1, first + p, r0, ui, nx)

        planes_of(lower, upper, nx, body)

    fill(own, 0, PLANES, 2)

    @pl.when(odd == 0)
    def _():
        fill(swap, 0, 2, 0)
        fill(near, 0, 2, 6)

    @pl.when(odd == 1)
    def _():
        fill(near, 2, 4, -2)
        fill(swap, 0, 2, 6)

    def smooth(p, block, q, r0, rows):
        sr, si = around(u, p, r0, zero)
        er = KEEP * block[0, q, rows] + sr
        ei = KEEP * block[1, q, rows] + si
        wr, wi = weight_of(block[2, q, rows])
        vr, vi = cmul(wr, wi, er, ei)
        put(u2, 0, p, r0, vr, nx)
        put(u2, 1, p, r0, vi, nx)
        return er, ei

    def inner(q, r0, rows):
        er, ei = smooth(2 + q, own, q, r0, rows)
        e1[0, q, rows] = er
        e1[1, q, rows] = ei

    planes_of(0, PLANES, nx, inner)

    def outer(block, q, p):
        planes_of(q, q + 1, nx, lambda q, r0, rows: smooth(p, block, q, r0, rows))

    @pl.when(odd == 0)
    def _():
        outer(swap, OUTER - 1, 1)
        outer(near, 0, 6)

    @pl.when(odd == 1)
    def _():
        outer(near, PLANES - 1, 1)
        outer(swap, 0, 6)

    half = nx // 2
    for q in range(PLANES // 2):
        for r0 in range(0, nx, CHUNK):
            rows = pl.ds(r0, CHUNK)
            total = [0.0, 0.0]
            for p in (2 * q, 2 * q + 1):
                s = around(u2, 2 + p, r0, zero)
                for c in range(2):
                    total[c] = total[c] + KEEP * e1[c, p, rows] + s[c]
            for c in range(2):
                tmp[q, c, rows] = total[c]
        out[pl.ds(half * q, half), :] = restrict_fine(tmp.at[q])
    out[pl.ds(2 * half, static.shape[0]), :] = static[...]


def static_kernel(at, own, orders, out, tmp, tmp1):
    nx, ny = own.shape[2:]
    half = nx // 2
    planes = []
    for q in range(PLANES // 2):
        for r0 in range(0, nx, CHUNK):
            rows = pl.ds(r0, CHUNK)
            below, above = shift_of(own[2, 2 * q, rows]), shift_of(own[2, 2 * q + 1, rows])
            for c in range(2):
                tmp[q, c, rows] = below[c] + above[c]
        shift = restrict_fine(tmp.at[q])
        out[pl.ds(half * q, half), :] = weights_packed(shift, ny // 2, H1)
        planes.append(shift)
    tmp1[...] = planes[0] + planes[1]
    pooled = tmp1[pl.ds(0, half // 2, stride=2), :] + tmp1[pl.ds(1, half // 2, stride=2), :]
    shift2 = dot(pooled, pool_level1(ny))
    out[pl.ds(2 * half, half // 2), :] = weights_packed(shift2, ny // 4, H2)
    out[pl.ds(2 * half + half // 2, 8), :] = jnp.broadcast_to(orders[...], (8, ny))


def coarse_shapes(group, nx, ny):
    n1 = (2 * group + 2 * PAD1, nx // 2 + 2 * HALO, ny)
    n2 = (group + 2 * PAD2, nx // 4 + 2 * HALO, ny)
    return [n1[:1] + (nx // 2, ny), n1, n1, n1, n1, n2[:1] + (nx // 4, ny), n2, n2, (nx // 2, ny), (group * (nx // 2), ny)]


def clear_edges(ref, pad, count):
    zero = jnp.zeros(ref.shape[1:], F32)
    top = ref.shape[0] - pad
    for k in range(count):
        ref[pad - 1 - k] = zero
        ref[top + k] = zero


def coarse_weights(me, masks, pieces, w1r, w1i, w2r, w2i):
    half, ny = w1r.shape[1:]
    quarter = half // 2
    for ref, pad in ((w1r, PAD1), (w1i, PAD1), (w2r, PAD2), (w2i, PAD2)):
        clear_edges(ref, pad, pad - 1)

    def expand(w, part):
        other = pltpu.roll(w, part, 1)
        real_lane = lanes(w.shape) % (2 * part) < part
        return jnp.where(real_lane, w, other), jnp.where(real_lane, -other, w)

    for mask, (piece, j) in zip(masks, pieces, strict=True):
        d = me ^ mask
        for k in range(2):
            wr, wi = expand(piece[j, pl.ds(half * (2 + k), half), :], ny // 2)
            w1r[PAD1 + 2 * d + k] = wr
            w1i[PAD1 + 2 * d + k] = wi
        wr, wi = expand(piece[j, pl.ds(4 * half, quarter), :], ny // 4)
        w2r[PAD2 + d] = wr
        w2i[PAD2 + d] = wi


def chunked(lower, count, most, body):
    size = max(n for n in range(1, most + 1) if count % n == 0)

    def step(k, carry):
        body(lower + k * size, size)
        return carry

    lax.fori_loop(0, count // size, step, 0)


def coarse_solve(me, zero, masks, pieces, reach, w1r, w1i, w2r, w2i, g1, u1, u2, v1, e1, g2, va, vb, tmp, pool, out):
    half, ny = tmp.shape
    quarter = half // 2
    group = len(masks)
    part1, part2 = ny // 2, ny // 4
    n1 = 2 * group
    clear_edges(g1, PAD1, PAD1 - 1)
    clear_edges(u1, PAD1, 1)
    clear_edges(u2, PAD1, 1)
    clear_edges(v1, PAD1, PAD1 - 1)
    clear_edges(va, PAD2, 1)
    clear_edges(vb, PAD2, PAD2 - 1)
    for mask, (piece, j) in zip(masks, pieces, strict=True):
        p = PAD1 + 2 * (me ^ mask)
        g = piece[j, pl.ds(0, 2 * half), :].reshape(2, half, ny)
        g1[pl.ds(p, 2)] = g
        put_packed(u1, p, 2, cmul_packed(w1r[pl.ds(p, 2)], w1i[pl.ds(p, 2)], g, part1))

    def pre(p, n):
        e = KEEP * g1[pl.ds(p, n)] + H1 * around_packed(u1, p, n, part1, zero)
        u = cmul_packed(w1r[pl.ds(p, n)], w1i[pl.ds(p, n)], e, part1)
        e1[pl.ds(p, n), pl.ds(0, half), :] = e
        put_packed(u2, p, n, u)
        put_packed(v1, p, n, mid_packed(u1, p, n) + u)

    chunked(PAD1, n1, 8, pre)

    def coarser(p, n):
        e = KEEP * e1[pl.ds(p, n), pl.ds(0, half), :] + H1 * around_packed(u2, p, n, part1, zero)
        e = e.reshape(n // 2, 2, half, ny)
        pairs = (e[:, 0] + e[:, 1]).reshape(n // 2 * half, ny)
        pool[pl.ds((p - PAD1) // 2 * half, n // 2 * half), :] = pairs

    chunked(PAD1, n1, 8, coarser)
    rows = group * quarter
    flat = pool[pl.ds(0, rows, stride=2), :] + pool[pl.ds(1, rows, stride=2), :]
    r2 = dot(flat, pool_level1(ny)).reshape(group, quarter, ny)
    inside = pl.ds(PAD2, group)
    g2[inside] = r2
    put_packed(va, PAD2, group, cmul_packed(w2r[inside], w2i[inside], r2, part2))
    for src, dst in ((va, vb), (vb, va), (va, vb)):

        def sweep(p, n, src=src, dst=dst):
            s = g2[pl.ds(p, n)] + H2 * around_packed(src, p, n, part2, zero)
            v = KEEP * mid_packed(src, p, n) + cmul_packed(w2r[pl.ds(p, n)], w2i[pl.ds(p, n)], s, part2)
            put_packed(dst, p, n, v)

        chunked(PAD2, group, 16, sweep)
    reach2 = (reach + 3) // 2
    count = 2 * reach2 + 1
    flat = mid_packed(vb, PAD2 + me - reach2, count).reshape(count * quarter, ny)
    r, c = iota2(ny, ny)
    spread = jnp.where(c // 2 == r, 1.0, 0.0).astype(F32)
    e2 = dot(flat, spread)
    pool[pl.ds(0, count * quarter, stride=2), :] = e2
    pool[pl.ds(1, count * quarter, stride=2), :] = e2
    base = PAD1 + 2 * (me - reach2)
    for k in range(count):
        add = pool[pl.ds(k * half, half), :]
        both = mid_packed(v1, base + 2 * k, 2) + add[None]
        put_packed(v1, base + 2 * k, 2, both)

    def post(src, p, n):
        s = g1[pl.ds(p, n)] + H1 * around_packed(src, p, n, part1, zero)
        return KEEP * mid_packed(src, p, n) + cmul_packed(w1r[pl.ds(p, n)], w1i[pl.ds(p, n)], s, part1)

    start = PAD1 + 2 * me

    def third(p, n):
        put_packed(u1, p, n, post(v1, p, n))

    def fourth(p, n):
        out[pl.ds(p - (start - reach), n)] = post(u1, p, n)

    chunked(start - reach - 1, 2 * reach + 4, 6, third)
    chunked(start - reach, 2 * reach + 2, 5, fourth)


def add_correction(ec, before, v, tmp, planes, nx):
    half, ny = ec.shape[1:]
    r, c = iota2(ny, 2 * ny)
    spread = jnp.where(c // 2 == r, 1.0, 0.0).astype(F32)

    def body(m, carry):
        k = 2 * m
        both = dot(ec[pl.ds(k, 2)].reshape(2 * half, ny), spread)
        for j in range(2):
            for c in range(2):
                e = both[j * half : (j + 1) * half, c * ny : (c + 1) * ny]
                tmp[j, c, pl.ds(0, half, stride=2), :] = e
                tmp[j, c, pl.ds(1, half, stride=2), :] = e
        for j in range(2):
            for c in range(2):
                for r0 in range(0, nx, CHUNK):
                    add = tmp[j, c, pl.ds(r0, CHUNK)]
                    for p in (2 * (k + j), 2 * (k + j) + 1):
                        put(v, c, p, r0, mid(before, c, p, r0) + add, nx)
        return carry

    lax.fori_loop(0, planes // 2, body, 0)


def ahead_kernel(at, own, near, swap, swap_outer, skip, far, f, weight, v, code, u):
    odd, zero = at[1], at[2]
    nx = own.shape[2]

    def fill(block, first):
        def body(q, r0, rows):
            p = first + q
            c = block[2, q, rows]
            wr, wi = weight_of(c)
            fr, fi = block[0, q, rows], block[1, q, rows]
            ur, ui = cmul(wr, wi, fr, fi)
            f[0, p, rows], f[1, p, rows] = fr, fi
            weight[0, p, rows], weight[1, p, rows] = wr, wi
            put(u, 0, p, r0, ur, nx)
            put(u, 1, p, r0, ui, nx)
            code[p, rows] = c

        planes_of(0, block.shape[1], nx, body)

    top = OWN + PLANES
    fill(own, OWN)
    fill(near, top - 2 * PLANES * odd)
    fill(swap, PLANES + 3 * OUTER * odd)
    fill(swap_outer, OUTER + 5 * OUTER * odd)
    fill(skip, (WINDOW - OUTER) * odd)
    fill(far, (WINDOW - OUTER) * (1 - odd))

    def pre(p, r0, rows):
        sr, si = around(u, p, r0, zero)
        er = KEEP * f[0, p, rows] + sr
        ei = KEEP * f[1, p, rows] + si
        vr, vi = cmul(weight[0, p, rows], weight[1, p, rows], er, ei)
        put(v, 0, p, r0, mid(u, 0, p, r0) + vr, nx)
        put(v, 1, p, r0, mid(u, 1, p, r0) + vi, nx)

    planes_of(1, WINDOW - 1, nx, pre, 7)


def second_kernel(masks, layout, at, f, weight, before, code, *refs):
    n = max(i for i, _ in layout) + 1
    gathered, refs = refs[:n], refs[n:]
    (direction, image, to_near, to_swap, pay, w1r, w1i, w2r, w2i), refs = refs[:9], refs[9:]
    u, u2, v, tmp, ec, e1 = refs[:6]
    coarse = refs[6:]
    me, odd, zero = at[0], at[1], at[2]
    nx, ny = f.shape[2:]
    pieces = [(gathered[i], j) for i, j in layout]
    coarse_weights(me, masks, pieces, w1r, w1i, w2r, w2i)
    coarse_solve(me, zero, masks, pieces, OWN // 2, w1r, w1i, w2r, w2i, *coarse, ec)
    add_correction(ec, before, v, tmp, WINDOW // 2, nx)

    def sweep(src, dst, p, r0, rows):
        sr, si = around(src, p, r0, zero)
        vr, vi = cmul(weight[0, p, rows], weight[1, p, rows], f[0, p, rows] + sr, f[1, p, rows] + si)
        put(dst, 0, p, r0, KEEP * mid(src, 0, p, r0) + vr, nx)
        put(dst, 1, p, r0, KEEP * mid(src, 1, p, r0) + vi, nx)

    planes_of(2, WINDOW - 2, nx, lambda *a: sweep(v, u, *a))
    planes_of(3, WINDOW - 3, nx, lambda *a: sweep(u, v, *a), 5)

    def apply(p, r0, rows):
        sr, si = around(v, p, r0, zero)
        c = code[p, rows]
        hr, hi = helm_of(c)
        vr, vi = mid(v, 0, p, r0), mid(v, 1, p, r0)
        ar, ai = cmul(hr, hi, vr, vi)
        ar = jnp.where(c > 0.0, ar + 6.0 * vr - sr, 0.0)
        ai = jnp.where(c > 0.0, ai + 6.0 * vi - si, 0.0)
        image[0, p - 4, rows] = ar
        image[1, p - 4, rows] = ai
        ur, ui = cmul(weight[0, p, rows], weight[1, p, rows], ar, ai)
        put(u, 0, p, r0, ur, nx)
        put(u, 1, p, r0, ui, nx)

    planes_of(4, WINDOW - 4, nx, apply)
    rho, cross_r, cross_i = 0.0, 0.0, 0.0
    for q in range(PLANES):
        for r0 in range(0, nx, CHUNK):
            rows = pl.ds(r0, CHUNK)
            fr, fi = f[0, OWN + q, rows], f[1, OWN + q, rows]
            ir, ii = image[0, OWN - 4 + q, rows], image[1, OWN - 4 + q, rows]
            rho = rho + fr * fr + fi * fi
            cross_r = cross_r + fr * ir + fi * ii
            cross_i = cross_i + fr * ii - fi * ir
            for c in range(2):
                direction[c, q, rows] = mid(v, c, OWN + q, r0)
    half = nx // 2
    row = lax.broadcasted_iota(jnp.int32, (8, ny), 0)
    sums = [jnp.sum(t, axis=0, keepdims=True) for t in (rho, cross_r, cross_i)]
    tail = jnp.where(row == 0, sums[0], jnp.where(row == 1, sums[1], jnp.where(row == 2, sums[2], 0.0)))
    pay[pl.ds(2 * half, 8), :] = tail

    def edges(q, r0, rows):
        for c in range(2):
            to_near[c, q, rows] = image[c, OWN - 4 + q + 2 * odd, rows]
            to_swap[c, q, rows] = image[c, OWN - 2 + q - 2 * odd, rows]

    planes_of(0, 2, nx, edges)

    def pre2(p, r0, rows):
        sr, si = around(u, p, r0, zero)
        er = KEEP * image[0, p - 4, rows] + sr
        ei = KEEP * image[1, p - 4, rows] + si
        vr, vi = cmul(weight[0, p, rows], weight[1, p, rows], er, ei)
        e1[0, p, rows], e1[1, p, rows] = er, ei
        put(u2, 0, p, r0, vr, nx)
        put(u2, 1, p, r0, vi, nx)

    planes_of(OWN - 1, OWN + PLANES + 1, nx, pre2, 6)
    for q in range(PLANES // 2):
        for r0 in range(0, nx, CHUNK):
            rows = pl.ds(r0, CHUNK)
            total = [0.0, 0.0]
            for k in range(2):
                p = OWN + 2 * q + k
                s = around(u2, p, r0, zero)
                for c in range(2):
                    total[c] = total[c] + KEEP * e1[c, p, rows] + s[c]
            for c in range(2):
                tmp[q, c, rows] = total[c]
        pay[pl.ds(half * q, half), :] = restrict_fine(tmp.at[q])


def widen_kernel(at, image, near, swap, weight, wide, smooth, u):
    odd, zero = at[1], at[2]
    nx = image.shape[2]

    def fill(block, first):
        def body(q, r0, rows):
            p = first + q
            fr, fi = block[0, q, rows], block[1, q, rows]
            ur, ui = cmul(weight[0, p + OUTER, rows], weight[1, p + OUTER, rows], fr, fi)
            wide[0, p, rows], wide[1, p, rows] = fr, fi
            put(u, 0, p, r0, ur, nx)
            put(u, 1, p, r0, ui, nx)

        planes_of(0, block.shape[1], nx, body)

    fill(image, 2)
    fill(near, 10 - 10 * odd)
    fill(swap, 10 * odd)

    def pre(p, r0, rows):
        sr, si = around(u, p, r0, zero)
        er = KEEP * wide[0, p, rows] + sr
        ei = KEEP * wide[1, p, rows] + si
        vr, vi = cmul(weight[0, p + OUTER, rows], weight[1, p + OUTER, rows], er, ei)
        put(smooth, 0, p, r0, mid(u, 0, p, r0) + vr, nx)
        put(smooth, 1, p, r0, mid(u, 1, p, r0) + vi, nx)

    planes_of(1, 11, nx, pre, 5)


def phase_kernel(masks, layout, row, at, *refs):
    n = max(i for i, _ in layout) + 1
    gathered = refs[:n]
    table, qrow, found = refs[n:]
    me = at[0]
    ny = found.shape[1]
    nx = table.shape[0] // 2
    for mask, (i, j) in zip(masks, layout, strict=True):
        found[pl.ds(me ^ mask, 1), :] = gathered[i][j, pl.ds(row, 1), :]
    low = lanes((1, ny)) < ny // 2
    x = lax.broadcasted_iota(jnp.int32, (nx, ny), 0)
    for pair in range(len(masks) // 2):
        even = found[pl.ds(2 * pair, 1), :]
        odd = found[pl.ds(2 * pair + 1, 1), :]
        p = jnp.where(low, even, pltpu.roll(odd, ny // 2, 1))
        q = jnp.where(low, pltpu.roll(even, ny // 2, 1), odd)
        turns = (x * p.astype(jnp.int32)) & (nx - 1)
        angle = turns.astype(F32) * (2.0 * math.pi / nx)
        table[pl.ds(0, nx), pl.ds(pair * ny, ny)] = jnp.cos(angle)
        table[pl.ds(nx, nx), pl.ds(pair * ny, ny)] = -jnp.sin(angle)
        qrow[:, pl.ds(pair * ny, ny)] = jnp.broadcast_to(q, (8, ny))


def third_kernel(
    masks, layout, at, own, direction, image, smooth2, weight, w1r, w1i, w2r, w2i, ytable, xtable, qrow, *refs
):
    n = max(i for i, _ in layout) + 1
    gathered, refs = refs[:n], refs[n:]
    (corrected, last_image, halfway, pay, alpha), refs = refs[:5], refs[5:]
    u, v, tmp, ec = refs[:4]
    coarse = refs[4:]
    me, zero = at[0], at[2]
    pieces = [(gathered[i], j) for i, j in layout]
    nx, ny = own.shape[2:]
    half = nx // 2
    coarse_solve(me, zero, masks, pieces, 2, w1r, w1i, w2r, w2i, *coarse, ec)
    add_correction(ec, smooth2, v, tmp, 6, nx)

    def sweep(src, dst, p, r0, rows):
        sr, si = around(src, p, r0, zero)
        wr, wi = weight[0, p + OUTER, rows], weight[1, p + OUTER, rows]
        vr, vi = cmul(wr, wi, image[0, p, rows] + sr, image[1, p, rows] + si)
        put(dst, 0, p, r0, KEEP * mid(src, 0, p, r0) + vr, nx)
        put(dst, 1, p, r0, KEEP * mid(src, 1, p, r0) + vi, nx)

    planes_of(2, 10, nx, lambda *a: sweep(v, u, *a))
    planes_of(3, 9, nx, lambda *a: sweep(u, v, *a))

    sums = 0.0
    for i, j in layout:
        sums = sums + gathered[i][j, pl.ds(2 * half, 8), :]
    rho, cr, ci = [jnp.sum(sums[k : k + 1], axis=1, keepdims=True) for k in range(3)]
    modulus = cr * cr + ci * ci
    ar = rho * cr / modulus
    ai = -rho * ci / modulus
    dots = [0.0, 0.0, 0.0]
    for q in range(PLANES):
        for r0 in range(0, nx, CHUNK):
            rows = pl.ds(r0, CHUNK)
            p = 4 + q
            sr, si = around(v, p, r0, zero)
            hr, hi = helm_of(own[2, q, rows])
            wr, wi = mid(v, 0, p, r0), mid(v, 1, p, r0)
            br, bi = cmul(hr, hi, wr, wi)
            br, bi = br + 6.0 * wr - sr, bi + 6.0 * wi - si
            ir, ii = image[0, p, rows], image[1, p, rows]
            br, bi = cmul(ar, ai, br, bi)
            lr, li = ir - br, ii - bi
            tr, ti = cmul(ar, ai, ir, ii)
            hr, hi = own[0, q, rows] - tr, own[1, q, rows] - ti
            xr, xi = cmul(ar, ai, wr, wi)
            corrected[0, q, rows], corrected[1, q, rows] = direction[0, q, rows] - xr, direction[1, q, rows] - xi
            last_image[0, q, rows], last_image[1, q, rows] = lr, li
            halfway[0, q, rows], halfway[1, q, rows] = hr, hi
            dots[0] = dots[0] + lr * hr + li * hi
            dots[1] = dots[1] + lr * hi - li * hr
            dots[2] = dots[2] + lr * lr + li * li
    dots = [jnp.sum(t, axis=0, keepdims=True) for t in dots]
    row = lax.broadcasted_iota(jnp.int32, (8, ny), 0)
    alpha[...] = jnp.where(row == 0, ar, ai)

    sign = jnp.where(lanes((nx, ny)) < ny // 2, -1.0, 1.0)
    stacked = []
    for field in (direction, corrected):
        plane = field[:, PLANES - 1].reshape(2 * nx, ny)
        m = lax.dot_general(
            ytable[...],
            plane,
            (((1,), (1,)), ((), ())),
            precision=lax.Precision.HIGHEST,
            preferred_element_type=F32,
        )
        t = m[:nx] + sign * pltpu.roll(m[nx:], nx, 1)
        stacked += [-sign * t, pltpu.roll(t, nx, 1)]
    spectrum = dot(jnp.concatenate(stacked, axis=0), xtable[...])
    scale = 1.0 / math.sqrt(nx * ny)
    at_row = lax.broadcasted_iota(jnp.int32, (nx, ny), 0).astype(F32) - ORD_HALF
    for pair in range(len(masks) // 2):
        chosen = at_row == qrow[0:1, pair * ny : (pair + 1) * ny]
        found = [
            scale
            * jnp.sum(
                jnp.where(chosen, spectrum[k * nx : (k + 1) * nx, pair * ny : (pair + 1) * ny], 0.0),
                axis=0,
                keepdims=True,
            )
            for k in range(4)
        ]
        block = 0.0
        for k, line in enumerate(found + dots):
            block = jnp.where(row == k, line, block)
        pay[2 * pair] = block
        pay[2 * pair + 1] = block


def last_kernel(at, direction, corrected, last_image, halfway, alpha, got, solution, residual, pupil):
    group = got.shape[0]
    nx, ny = direction.shape[2:]
    total = got[0]
    for k in range(1, group):
        total = total + got[k]
    along_r, along_i, norm = [jnp.sum(total[k : k + 1], axis=1, keepdims=True) for k in (4, 5, 6)]
    wr = along_r / norm
    wi = along_i / norm
    ar = alpha[0:1, 0:1]
    ai = alpha[1:2, 0:1]
    for q in range(PLANES):
        for r0 in range(0, nx, CHUNK):
            rows = pl.ds(r0, CHUNK)
            xr, xi = cmul(ar, ai, direction[0, q, rows], direction[1, q, rows])
            yr, yi = cmul(wr, wi, corrected[0, q, rows], corrected[1, q, rows])
            solution[0, q, rows], solution[1, q, rows] = xr + yr, xi + yi
            zr, zi = cmul(wr, wi, last_image[0, q, rows], last_image[1, q, rows])
            residual[0, q, rows], residual[1, q, rows] = halfway[0, q, rows] - zr, halfway[1, q, rows] - zi
    tip = got[group - 1]
    xr, xi = cmul(ar, ai, tip[0:1], tip[1:2])
    yr, yi = cmul(wr, wi, tip[2:3], tip[3:4])
    both = jnp.concatenate([xr + yr, xi + yi] * 4, axis=0)
    both = jnp.where(at[1] == 1, pltpu.roll(both, ny // 2, 1), both)
    pupil[...] = both[:2, : ny // 2]


def exchange(x, mask, group):
    return lax.ppermute(x, "gz", [(i, i ^ mask) for i in range(group)])


def swap_across(x, group):
    pairs = []
    for i in range(1, group - 1, 2):
        pairs += [(i, i + 1), (i + 1, i)]
    return lax.ppermute(x, "gz", pairs)


def skip_across(x, group):
    pairs = []
    for i in range(group):
        target = i + 2 if i % 2 == 0 else i - 2
        if 0 <= target < group:
            pairs.append((i, target))
    return lax.ppermute(x, "gz", pairs)


def stages_of(group):
    stages = [[1]]
    stride = 2
    left = group // 2
    if left.bit_length() % 2 == 0:
        stages.insert(0, [stride])
        stride, left = 2 * stride, left // 2
    while left > 1:
        stages.insert(0, [stride, 2 * stride, 3 * stride])
        stride, left = 4 * stride, left // 4
    return stages


def gather(x, group):
    have, masks = x[None], [0]
    stages = stages_of(group)
    for masks_now in stages[:-1]:
        got = [exchange(have, m, group) for m in masks_now]
        masks = masks + [k ^ m for m in masks_now for k in masks]
        have = jnp.concatenate([have] + got, axis=0)
    (m,) = stages[-1]
    other = exchange(have, m, group)
    count = len(masks)
    layout = [(0, j) for j in range(count)] + [(1, j) for j in range(count)]
    return [have, other], masks + [k ^ m for k in masks], layout


def y_phases(nx, ny):
    q = np.arange(nx) - ORD_HALF
    turns = (q[:, None] * np.arange(ny)[None, :]) % ny
    angle = turns.astype(np.float64) * (2.0 * np.pi / ny)
    return np.concatenate([np.cos(angle), -np.sin(angle)], axis=0).astype(np.float32)


def on_device(source_term, material, orders):
    group = lax.axis_size("gz")
    _, planes, nx, ny = source_term.shape
    assert planes == PLANES and 2 * nx == ny and 2 * orders.shape[1] == ny
    me = lax.axis_index("gz")
    at = jnp.stack([me, me % 2, me * 0]).astype(jnp.int32)
    half = nx // 2

    fine = (2, PLANES, nx, ny)
    half_block = (3, OUTER, nx, ny)
    own, inner, outer = call(
        pack_kernel, [(3, PLANES, nx, ny), half_block, half_block], [at, source_term, material], []
    )
    swap = swap_across(inner, group)
    near = exchange(own, 1, group)
    swap_outer = swap_across(outer, group)
    skip = skip_across(outer, group)
    far = exchange(swap, 1, group)
    order_row = orders.astype(F32).reshape(1, ny)
    tall = nx + 2 * HALO
    (pay0,) = call(static_kernel, [(2 * half + half // 2 + 8, ny)], [at, own, order_row], [(2, 2, nx, ny), (half, ny)])
    (pay1,) = call(
        first_kernel,
        [(4 * half + half // 2 + 8, ny)],
        [at, own, near, swap, pay0],
        [(2, 8, tall, ny), fine, (2, 8, tall, ny), (2, 2, nx, ny)],
    )
    gathered1, masks, layout = gather(pay1, group)
    window = (2, WINDOW, nx, ny)
    haloed = (2, WINDOW, tall, ny)
    shapes1 = (2 * group + 2 * PAD1, half, ny)
    shapes2 = (group + 2 * PAD2, half // 2, ny)
    f, weight, before, code = call(
        ahead_kernel, [window, window, haloed, (WINDOW, nx, ny)], [at, own, near, swap, swap_outer, skip, far], [haloed]
    )
    edge = (2, 2, nx, ny)
    direction, image, to_near, to_swap, pay2, w1r, w1i, w2r, w2i = call(
        functools.partial(second_kernel, masks, layout),
        [
            fine,
            (2, WINDOW - 8, nx, ny),
            edge,
            edge,
            (2 * half + 8, ny),
            shapes1,
            shapes1,
            shapes2,
            shapes2,
        ],
        [at, f, weight, before, code, *gathered1],
        [haloed, haloed, haloed, (2, 2, nx, ny), (WINDOW // 2, half, ny), window] + coarse_shapes(group, nx, ny),
    )
    near2 = exchange(to_near, 1, group)
    swap2 = swap_across(to_swap, group)
    wide, smooth2 = call(
        widen_kernel, [(2, 12, nx, ny), (2, 12, tall, ny)], [at, image, near2, swap2, weight], [(2, 12, tall, ny)]
    )
    xtable, qrow = call(
        functools.partial(phase_kernel, masks, layout, 4 * half + half // 2),
        [(2 * nx, group * ny // 2), (8, group * ny // 2)],
        [at, *gathered1],
        [(group, ny)],
    )
    gathered2, masks, layout = gather(pay2, group)
    corrected, last_image, halfway, pay3, alpha = call(
        functools.partial(third_kernel, masks, layout),
        [fine, fine, fine, (group, 8, ny), (8, ny)],
        [
            at,
            own,
            direction,
            wide,
            smooth2,
            weight,
            w1r,
            w1i,
            w2r,
            w2i,
            jnp.asarray(y_phases(nx, ny)),
            xtable,
            qrow,
            *gathered2,
        ],
        [(2, 12, tall, ny), (2, 12, tall, ny), (2, 2, nx, ny), (6, half, ny)] + coarse_shapes(group, nx, ny),
    )
    got = lax.all_to_all(pay3, "gz", 0, 0)
    solution, residual, pupil = call(
        last_kernel, [fine, fine, (2, ny // 2)], [at, direction, corrected, last_image, halfway, alpha, got], []
    )
    return solution, residual, pupil


def solution(mesh):
    return jax.shard_map(
        on_device,
        mesh=mesh,
        in_specs=(
            P(None, ("clip", "gz"), None, None),
            P(("clip", "gz"), None, None),
            P(None, "gz"),
        ),
        out_specs=(
            P(None, ("clip", "gz"), None, None),
            P(None, ("clip", "gz"), None, None),
            P(None, ("clip", "gz")),
        ),
        check_vma=False,
    )
```

```python
import functools
import math

import jax
import jax.numpy as jnp
import numpy as np
from jax import lax
from jax.experimental import pallas as pl
from jax.experimental.pallas import tpu as pltpu
from jax.sharding import PartitionSpec as P


ORD_HALF = 22
HELM_TABLE = ((-0.5, 0.0), (1.0, -1.4), (-1.2, 0.0))
SHIFT_TABLE = ((-0.5, -0.25), (1.0, -0.25 * math.sqrt(11.84)), (-1.2, -0.6))
RELAX = 0.8
KEEP = 1.0 - RELAX
PLANES = 4
OUTER = 2
OWN = PLANES + OUTER
WINDOW = PLANES + 2 * OWN
PAD1 = 8
PAD2 = 4
H1 = 0.25
H2 = 0.0625
F32 = jnp.float32
VMEM_LIMIT = 28 * 2**20

WEIGHTS = tuple(RELAX / complex(6.0 + s[0], s[1]) for s in SHIFT_TABLE)


def pick(code, values):
    return jnp.where(
        code == 1.0,
        values[0],
        jnp.where(code == 2.0, values[1], jnp.where(code == 3.0, values[2], 0.0)),
    )


def weight_of(code):
    return pick(code, [w.real for w in WEIGHTS]), pick(code, [w.imag for w in WEIGHTS])


def shift_of(code):
    return pick(code, [s[0] for s in SHIFT_TABLE]), pick(code, [s[1] for s in SHIFT_TABLE])


def helm_of(code):
    return pick(code, [s[0] for s in HELM_TABLE]), pick(code, [s[1] for s in HELM_TABLE])


def cmul(ar, ai, br, bi):
    return ar * br - ai * bi, ar * bi + ai * br


HALO = 8
CHUNK = 16


def put(ref, c, p, r0, value, nx):
    n = value.shape[0]
    ref[c, p, pl.ds(HALO + r0, n), :] = value
    if r0 == 0:
        ref[c, p, pl.ds(HALO + nx, 1), :] = value[:1]
    if r0 + n == nx:
        ref[c, p, pl.ds(HALO - 1, 1), :] = value[n - 1 :]


def mid(ref, c, p, r0, n=CHUNK):
    return ref[c, p, pl.ds(HALO + r0, n), :]


def around(ref, p, r0, zero):
    sums = []
    for c in range(2):
        m = mid(ref, c, p, r0)
        ny = m.shape[1]
        total = mid(ref, c, p - 1, r0) + mid(ref, c, p + 1, r0)
        total = total + ref[c, p, pl.ds(HALO - 1 + r0 + zero, CHUNK), :]
        total = total + ref[c, p, pl.ds(HALO + 1 + r0 + zero, CHUNK), :]
        total = total + pltpu.roll(m, 1, 1) + pltpu.roll(m, ny - 1, 1)
        sums.append(total)
    return sums


def planes_of(lower, upper, nx, body, most=4):
    size = max(n for n in range(1, most + 1) if (upper - lower) % n == 0)

    def step(k, carry):
        for j in range(size):
            for r0 in range(0, nx, CHUNK):
                body(lower + k * size + j, r0, pl.ds(r0, CHUNK))
        return carry

    lax.fori_loop(0, (upper - lower) // size, step, 0)


def lanes(shape):
    return lax.broadcasted_iota(jnp.int32, shape, len(shape) - 1)


def put_packed(ref, p, count, value):
    n = value.shape[1]
    ref[pl.ds(p, count), pl.ds(HALO, n), :] = value
    ref[pl.ds(p, count), pl.ds(HALO + n, 1), :] = value[:, :1]
    ref[pl.ds(p, count), pl.ds(HALO - 1, 1), :] = value[:, n - 1 :]


def mid_packed(ref, p, count):
    return ref[pl.ds(p, count), pl.ds(HALO, ref.shape[1] - 2 * HALO), :]


def around_packed(ref, p, count, part, zero):
    m = mid_packed(ref, p, count)
    n, width = m.shape[1:]
    total = mid_packed(ref, p - 1, count) + mid_packed(ref, p + 1, count)
    total = total + ref[pl.ds(p, count), pl.ds(HALO - 1 + zero, n), :]
    total = total + ref[pl.ds(p, count), pl.ds(HALO + 1 + zero, n), :]
    at = lanes((1, 1, width)) % part
    before = jnp.where(at == 0, pltpu.roll(m, width + 1 - part, 2), pltpu.roll(m, 1, 2))
    after = jnp.where(at == part - 1, pltpu.roll(m, part - 1, 2), pltpu.roll(m, width - 1, 2))
    return total + before + after


def cmul_packed(wr, wi, g, part):
    return wr * g + wi * pltpu.roll(g, part, g.ndim - 1)


def weights_packed(shift, part, factor):
    other = pltpu.roll(shift, part, 1)
    real_lane = lanes(shift.shape) % (2 * part) < part
    dr = 6.0 * factor + jnp.where(real_lane, shift, other)
    di = jnp.where(real_lane, other, shift)
    scale = RELAX / (dr * dr + di * di)
    return jnp.where(real_lane, dr, -di) * scale


def dot_exact(a, b):
    high = a.astype(jnp.bfloat16)
    low = (a - high.astype(F32)).astype(jnp.bfloat16)
    b = b.astype(jnp.bfloat16)
    both = jnp.concatenate([high, low], axis=1)
    return jnp.dot(both, jnp.concatenate([b, b], axis=0), preferred_element_type=F32)


def iota2(rows, cols):
    return (
        lax.broadcasted_iota(jnp.int32, (rows, cols), 0),
        lax.broadcasted_iota(jnp.int32, (rows, cols), 1),
    )


def restrict_fine(tmp):
    nx, ny = tmp.shape[1:]
    half = nx // 2
    rows = [tmp[c, pl.ds(0, half, stride=2), :] + tmp[c, pl.ds(1, half, stride=2), :] for c in range(2)]
    r, c = iota2(2 * ny, ny)
    pool = jnp.where(r // 2 == c, 0.125, 0.0).astype(F32)
    return dot_exact(jnp.concatenate(rows, axis=1), pool)


def pool_level1(ny):
    r, c = iota2(ny, ny)
    return jnp.where(r // 2 == c % (ny // 2), 0.125, 0.0).astype(F32)


def full(shape_dtype):
    return jax.ShapeDtypeStruct(shape_dtype, F32)


VM = pl.BlockSpec(memory_space=pltpu.VMEM)
SM = pl.BlockSpec(memory_space=pltpu.SMEM)


def call(body, outs, inputs, scratch):
    size = sum(4 * math.prod(x.shape) for x in inputs) + sum(4 * math.prod(o) for o in outs)
    return pl.pallas_call(
        body,
        out_shape=[full(o) for o in outs],
        in_specs=[SM] + [VM] * (len(inputs) - 1),
        out_specs=[VM] * len(outs),
        scratch_shapes=[pltpu.VMEM(s, F32) for s in scratch],
        compiler_params=pltpu.CompilerParams(vmem_limit_bytes=VMEM_LIMIT),
        cost_estimate=pl.CostEstimate(flops=40 * size, bytes_accessed=size, transcendentals=0),
    )(*inputs)


def pack_kernel(at, source, material, own, inner, outer):
    odd = at[1]
    nx = source.shape[2]

    def join(p, r0, rows):
        for c in range(2):
            own[c, p, rows] = source[c, p, rows]
        own[2, p, rows] = (material[p, rows] + 1).astype(F32)

    planes_of(0, PLANES, nx, join)

    def halves(p, r0, rows):
        for c in range(3):
            inner[c, p, rows] = own[c, p + OUTER * odd, rows]
            outer[c, p, rows] = own[c, p + OUTER * (1 - odd), rows]

    planes_of(0, OUTER, nx, halves)


def first_kernel(at, own, near, swap, static, out, u, e1, u2, tmp):
    odd, zero = at[1], at[2]
    nx, _ = own.shape[2:]

    def fill(block, lower, upper, first):
        def body(p, r0, rows):
            wr, wi = weight_of(block[2, p, rows])
            ur, ui = cmul(wr, wi, block[0, p, rows], block[1, p, rows])
            put(u, 0, first + p, r0, ur, nx)
            put(u, 1, first + p, r0, ui, nx)

        planes_of(lower, upper, nx, body)

    fill(own, 0, PLANES, 2)

    @pl.when(odd == 0)
    def _():
        fill(swap, 0, 2, 0)
        fill(near, 0, 2, 6)

    @pl.when(odd == 1)
    def _():
        fill(near, 2, 4, -2)
        fill(swap, 0, 2, 6)

    def smooth(p, block, q, r0, rows):
        sr, si = around(u, p, r0, zero)
        er = KEEP * block[0, q, rows] + sr
        ei = KEEP * block[1, q, rows] + si
        wr, wi = weight_of(block[2, q, rows])
        vr, vi = cmul(wr, wi, er, ei)
        put(u2, 0, p, r0, vr, nx)
        put(u2, 1, p, r0, vi, nx)
        return er, ei

    def inner(q, r0, rows):
        er, ei = smooth(2 + q, own, q, r0, rows)
        e1[0, q, rows] = er
        e1[1, q, rows] = ei

    planes_of(0, PLANES, nx, inner)

    def outer(block, q, p):
        planes_of(q, q + 1, nx, lambda q, r0, rows: smooth(p, block, q, r0, rows))

    @pl.when(odd == 0)
    def _():
        outer(swap, OUTER - 1, 1)
        outer(near, 0, 6)

    @pl.when(odd == 1)
    def _():
        outer(near, PLANES - 1, 1)
        outer(swap, 0, 6)

    half = nx // 2
    for q in range(PLANES // 2):
        for r0 in range(0, nx, CHUNK):
            rows = pl.ds(r0, CHUNK)
            total = [0.0, 0.0]
            for p in (2 * q, 2 * q + 1):
                s = around(u2, 2 + p, r0, zero)
                for c in range(2):
                    total[c] = total[c] + KEEP * e1[c, p, rows] + s[c]
            for c in range(2):
                tmp[q, c, rows] = total[c]
        out[pl.ds(half * q, half), :] = restrict_fine(tmp.at[q])
    out[pl.ds(2 * half, static.shape[0]), :] = static[...]


def static_kernel(at, own, orders, out, tmp, tmp1):
    nx, ny = own.shape[2:]
    half = nx // 2
    planes = []
    for q in range(PLANES // 2):
        for r0 in range(0, nx, CHUNK):
            rows = pl.ds(r0, CHUNK)
            below, above = shift_of(own[2, 2 * q, rows]), shift_of(own[2, 2 * q + 1, rows])
            for c in range(2):
                tmp[q, c, rows] = below[c] + above[c]
        shift = restrict_fine(tmp.at[q])
        out[pl.ds(half * q, half), :] = weights_packed(shift, ny // 2, H1)
        planes.append(shift)
    tmp1[...] = planes[0] + planes[1]
    pooled = tmp1[pl.ds(0, half // 2, stride=2), :] + tmp1[pl.ds(1, half // 2, stride=2), :]
    shift2 = dot_exact(pooled, pool_level1(ny))
    out[pl.ds(2 * half, half // 2), :] = weights_packed(shift2, ny // 4, H2)
    wanted = orders[...].astype(F32)
    line = jnp.concatenate([wanted[0:1], wanted[1:2]], axis=1)
    out[pl.ds(2 * half + half // 2, 8), :] = jnp.broadcast_to(line, (8, ny))


def coarse_shapes(group, nx, ny):
    n1 = (2 * group + 2 * PAD1, nx // 2 + 2 * HALO, ny)
    n2 = (group + 2 * PAD2, nx // 4 + 2 * HALO, ny)
    return [n1[:1] + (nx // 2, ny), n1, n1, n1, n1, n2[:1] + (nx // 4, ny), n2, n2, (nx // 2, ny), (group * (nx // 2), ny)]


def clear_edges(ref, pad, count):
    zero = jnp.zeros(ref.shape[1:], F32)
    top = ref.shape[0] - pad
    for k in range(count):
        ref[pad - 1 - k] = zero
        ref[top + k] = zero


def coarse_weights(me, masks, pieces, w1r, w1i, w2r, w2i):
    half, ny = w1r.shape[1:]
    quarter = half // 2
    for ref, pad in ((w1r, PAD1), (w1i, PAD1), (w2r, PAD2), (w2i, PAD2)):
        clear_edges(ref, pad, pad - 1)

    def expand(w, part):
        other = pltpu.roll(w, part, 1)
        real_lane = lanes(w.shape) % (2 * part) < part
        return jnp.where(real_lane, w, other), jnp.where(real_lane, -other, w)

    for mask, (piece, j) in zip(masks, pieces, strict=True):
        d = me ^ mask
        for k in range(2):
            wr, wi = expand(piece[j, pl.ds(half * (2 + k), half), :], ny // 2)
            w1r[PAD1 + 2 * d + k] = wr
            w1i[PAD1 + 2 * d + k] = wi
        wr, wi = expand(piece[j, pl.ds(4 * half, quarter), :], ny // 4)
        w2r[PAD2 + d] = wr
        w2i[PAD2 + d] = wi


def chunked(lower, count, most, body):
    size = max(n for n in range(1, most + 1) if count % n == 0)

    def step(k, carry):
        body(lower + k * size, size)
        return carry

    lax.fori_loop(0, count // size, step, 0)


def coarse_solve(me, zero, masks, pieces, reach, w1r, w1i, w2r, w2i, g1, u1, u2, v1, e1, g2, va, vb, tmp, pool, out):
    half, ny = tmp.shape
    quarter = half // 2
    group = len(masks)
    part1, part2 = ny // 2, ny // 4
    n1 = 2 * group
    clear_edges(g1, PAD1, PAD1 - 1)
    clear_edges(u1, PAD1, 1)
    clear_edges(u2, PAD1, 1)
    clear_edges(v1, PAD1, PAD1 - 1)
    clear_edges(va, PAD2, 1)
    clear_edges(vb, PAD2, PAD2 - 1)
    for mask, (piece, j) in zip(masks, pieces, strict=True):
        p = PAD1 + 2 * (me ^ mask)
        g = piece[j, pl.ds(0, 2 * half), :].reshape(2, half, ny)
        g1[pl.ds(p, 2)] = g
        put_packed(u1, p, 2, cmul_packed(w1r[pl.ds(p, 2)], w1i[pl.ds(p, 2)], g, part1))

    def pre(p, n):
        e = KEEP * g1[pl.ds(p, n)] + H1 * around_packed(u1, p, n, part1, zero)
        u = cmul_packed(w1r[pl.ds(p, n)], w1i[pl.ds(p, n)], e, part1)
        e1[pl.ds(p, n), pl.ds(0, half), :] = e
        put_packed(u2, p, n, u)
        put_packed(v1, p, n, mid_packed(u1, p, n) + u)

    chunked(PAD1, n1, 8, pre)

    def coarser(p, n):
        e = KEEP * e1[pl.ds(p, n), pl.ds(0, half), :] + H1 * around_packed(u2, p, n, part1, zero)
        e = e.reshape(n // 2, 2, half, ny)
        pairs = (e[:, 0] + e[:, 1]).reshape(n // 2 * half, ny)
        pool[pl.ds((p - PAD1) // 2 * half, n // 2 * half), :] = pairs

    chunked(PAD1, n1, 8, coarser)
    rows = group * quarter
    flat = pool[pl.ds(0, rows, stride=2), :] + pool[pl.ds(1, rows, stride=2), :]
    r2 = dot_exact(flat, pool_level1(ny)).reshape(group, quarter, ny)
    inside = pl.ds(PAD2, group)
    g2[inside] = r2
    put_packed(va, PAD2, group, cmul_packed(w2r[inside], w2i[inside], r2, part2))
    for src, dst in ((va, vb), (vb, va), (va, vb)):

        def sweep(p, n, src=src, dst=dst):
            s = g2[pl.ds(p, n)] + H2 * around_packed(src, p, n, part2, zero)
            v = KEEP * mid_packed(src, p, n) + cmul_packed(w2r[pl.ds(p, n)], w2i[pl.ds(p, n)], s, part2)
            put_packed(dst, p, n, v)

        chunked(PAD2, group, 16, sweep)
    reach2 = (reach + 3) // 2
    count = 2 * reach2 + 1
    flat = mid_packed(vb, PAD2 + me - reach2, count).reshape(count * quarter, ny)
    r, c = iota2(ny, ny)
    spread = jnp.where(c // 2 == r, 1.0, 0.0).astype(F32)
    e2 = dot_exact(flat, spread)
    pool[pl.ds(0, count * quarter, stride=2), :] = e2
    pool[pl.ds(1, count * quarter, stride=2), :] = e2
    base = PAD1 + 2 * (me - reach2)
    for k in range(count):
        add = pool[pl.ds(k * half, half), :]
        both = mid_packed(v1, base + 2 * k, 2) + add[None]
        put_packed(v1, base + 2 * k, 2, both)

    def post(src, p, n):
        s = g1[pl.ds(p, n)] + H1 * around_packed(src, p, n, part1, zero)
        return KEEP * mid_packed(src, p, n) + cmul_packed(w1r[pl.ds(p, n)], w1i[pl.ds(p, n)], s, part1)

    start = PAD1 + 2 * me

    def third(p, n):
        put_packed(u1, p, n, post(v1, p, n))

    def fourth(p, n):
        out[pl.ds(p - (start - reach), n)] = post(u1, p, n)

    chunked(start - reach - 1, 2 * reach + 4, 6, third)
    chunked(start - reach, 2 * reach + 2, 5, fourth)


def add_correction(ec, before, v, tmp, planes, nx):
    half, ny = ec.shape[1:]
    r, c = iota2(ny, 2 * ny)
    spread = jnp.where(c // 2 == r, 1.0, 0.0).astype(F32)

    def body(m, carry):
        k = 2 * m
        both = dot_exact(ec[pl.ds(k, 2)].reshape(2 * half, ny), spread)
        for j in range(2):
            for c in range(2):
                e = both[j * half : (j + 1) * half, c * ny : (c + 1) * ny]
                tmp[j, c, pl.ds(0, half, stride=2), :] = e
                tmp[j, c, pl.ds(1, half, stride=2), :] = e
        for j in range(2):
            for c in range(2):
                for r0 in range(0, nx, CHUNK):
                    add = tmp[j, c, pl.ds(r0, CHUNK)]
                    for p in (2 * (k + j), 2 * (k + j) + 1):
                        put(v, c, p, r0, mid(before, c, p, r0) + add, nx)
        return carry

    lax.fori_loop(0, planes // 2, body, 0)


def ahead_kernel(at, own, near, swap, swap_outer, skip, far, f, weight, v, code, u):
    odd, zero = at[1], at[2]
    nx = own.shape[2]

    def fill(block, first):
        def body(q, r0, rows):
            p = first + q
            c = block[2, q, rows]
            wr, wi = weight_of(c)
            fr, fi = block[0, q, rows], block[1, q, rows]
            ur, ui = cmul(wr, wi, fr, fi)
            f[0, p, rows], f[1, p, rows] = fr, fi
            weight[0, p, rows], weight[1, p, rows] = wr, wi
            put(u, 0, p, r0, ur, nx)
            put(u, 1, p, r0, ui, nx)
            code[p, rows] = c

        planes_of(0, block.shape[1], nx, body)

    top = OWN + PLANES
    fill(own, OWN)
    fill(near, top - 2 * PLANES * odd)
    fill(swap, PLANES + 3 * OUTER * odd)
    fill(swap_outer, OUTER + 5 * OUTER * odd)
    fill(skip, (WINDOW - OUTER) * odd)
    fill(far, (WINDOW - OUTER) * (1 - odd))

    def pre(p, r0, rows):
        sr, si = around(u, p, r0, zero)
        er = KEEP * f[0, p, rows] + sr
        ei = KEEP * f[1, p, rows] + si
        vr, vi = cmul(weight[0, p, rows], weight[1, p, rows], er, ei)
        put(v, 0, p, r0, mid(u, 0, p, r0) + vr, nx)
        put(v, 1, p, r0, mid(u, 1, p, r0) + vi, nx)

    planes_of(1, WINDOW - 1, nx, pre, 7)


def second_kernel(masks, layout, at, f, weight, before, code, *refs):
    n = max(i for i, _ in layout) + 1
    gathered, refs = refs[:n], refs[n:]
    (direction, image, to_near, to_swap, pay, w1r, w1i, w2r, w2i), refs = refs[:9], refs[9:]
    u, u2, v, tmp, ec, e1 = refs[:6]
    coarse = refs[6:]
    me, odd, zero = at[0], at[1], at[2]
    nx, ny = f.shape[2:]
    pieces = [(gathered[i], j) for i, j in layout]
    coarse_weights(me, masks, pieces, w1r, w1i, w2r, w2i)
    coarse_solve(me, zero, masks, pieces, OWN // 2, w1r, w1i, w2r, w2i, *coarse, ec)
    add_correction(ec, before, v, tmp, WINDOW // 2, nx)

    def sweep(src, dst, p, r0, rows):
        sr, si = around(src, p, r0, zero)
        vr, vi = cmul(weight[0, p, rows], weight[1, p, rows], f[0, p, rows] + sr, f[1, p, rows] + si)
        put(dst, 0, p, r0, KEEP * mid(src, 0, p, r0) + vr, nx)
        put(dst, 1, p, r0, KEEP * mid(src, 1, p, r0) + vi, nx)

    planes_of(2, WINDOW - 2, nx, lambda *a: sweep(v, u, *a))
    planes_of(3, WINDOW - 3, nx, lambda *a: sweep(u, v, *a), 5)

    def apply(p, r0, rows):
        sr, si = around(v, p, r0, zero)
        c = code[p, rows]
        hr, hi = helm_of(c)
        vr, vi = mid(v, 0, p, r0), mid(v, 1, p, r0)
        ar, ai = cmul(hr, hi, vr, vi)
        ar = jnp.where(c > 0.0, ar + 6.0 * vr - sr, 0.0)
        ai = jnp.where(c > 0.0, ai + 6.0 * vi - si, 0.0)
        image[0, p - 4, rows] = ar
        image[1, p - 4, rows] = ai
        ur, ui = cmul(weight[0, p, rows], weight[1, p, rows], ar, ai)
        put(u, 0, p, r0, ur, nx)
        put(u, 1, p, r0, ui, nx)

    planes_of(4, WINDOW - 4, nx, apply)
    rho, cross_r, cross_i = 0.0, 0.0, 0.0
    for q in range(PLANES):
        for r0 in range(0, nx, CHUNK):
            rows = pl.ds(r0, CHUNK)
            fr, fi = f[0, OWN + q, rows], f[1, OWN + q, rows]
            ir, ii = image[0, OWN - 4 + q, rows], image[1, OWN - 4 + q, rows]
            rho = rho + fr * fr + fi * fi
            cross_r = cross_r + fr * ir + fi * ii
            cross_i = cross_i + fr * ii - fi * ir
            for c in range(2):
                direction[c, q, rows] = mid(v, c, OWN + q, r0)
    half = nx // 2
    row = lax.broadcasted_iota(jnp.int32, (8, ny), 0)
    sums = [jnp.sum(t, axis=0, keepdims=True) for t in (rho, cross_r, cross_i)]
    tail = jnp.where(row == 0, sums[0], jnp.where(row == 1, sums[1], jnp.where(row == 2, sums[2], 0.0)))
    pay[pl.ds(2 * half, 8), :] = tail

    def edges(q, r0, rows):
        for c in range(2):
            to_near[c, q, rows] = image[c, OWN - 4 + q + 2 * odd, rows]
            to_swap[c, q, rows] = image[c, OWN - 2 + q - 2 * odd, rows]

    planes_of(0, 2, nx, edges)

    def pre2(p, r0, rows):
        sr, si = around(u, p, r0, zero)
        er = KEEP * image[0, p - 4, rows] + sr
        ei = KEEP * image[1, p - 4, rows] + si
        vr, vi = cmul(weight[0, p, rows], weight[1, p, rows], er, ei)
        e1[0, p, rows], e1[1, p, rows] = er, ei
        put(u2, 0, p, r0, vr, nx)
        put(u2, 1, p, r0, vi, nx)

    planes_of(OWN - 1, OWN + PLANES + 1, nx, pre2, 6)
    for q in range(PLANES // 2):
        for r0 in range(0, nx, CHUNK):
            rows = pl.ds(r0, CHUNK)
            total = [0.0, 0.0]
            for k in range(2):
                p = OWN + 2 * q + k
                s = around(u2, p, r0, zero)
                for c in range(2):
                    total[c] = total[c] + KEEP * e1[c, p, rows] + s[c]
            for c in range(2):
                tmp[q, c, rows] = total[c]
        pay[pl.ds(half * q, half), :] = restrict_fine(tmp.at[q])


def widen_kernel(at, image, near, swap, weight, wide, smooth, u):
    odd, zero = at[1], at[2]
    nx = image.shape[2]

    def fill(block, first):
        def body(q, r0, rows):
            p = first + q
            fr, fi = block[0, q, rows], block[1, q, rows]
            ur, ui = cmul(weight[0, p + OUTER, rows], weight[1, p + OUTER, rows], fr, fi)
            wide[0, p, rows], wide[1, p, rows] = fr, fi
            put(u, 0, p, r0, ur, nx)
            put(u, 1, p, r0, ui, nx)

        planes_of(0, block.shape[1], nx, body)

    fill(image, 2)
    fill(near, 10 - 10 * odd)
    fill(swap, 10 * odd)

    def pre(p, r0, rows):
        sr, si = around(u, p, r0, zero)
        er = KEEP * wide[0, p, rows] + sr
        ei = KEEP * wide[1, p, rows] + si
        vr, vi = cmul(weight[0, p + OUTER, rows], weight[1, p + OUTER, rows], er, ei)
        put(smooth, 0, p, r0, mid(u, 0, p, r0) + vr, nx)
        put(smooth, 1, p, r0, mid(u, 1, p, r0) + vi, nx)

    planes_of(1, 11, nx, pre, 5)


def phase_kernel(masks, layout, row, at, ytable, direction, *refs):
    n = max(i for i, _ in layout) + 1
    gathered = refs[:n]
    table, qrow, picks, found = refs[n:]
    me = at[0]
    ny = found.shape[1]
    nx = table.shape[0] // 6
    for mask, (i, j) in zip(masks, layout, strict=True):
        found[pl.ds(me ^ mask, 1), :] = gathered[i][j, pl.ds(row, 1), :]
    low = lanes((1, ny)) < ny // 2
    x = lax.broadcasted_iota(jnp.int32, (nx, ny), 0)
    for pair in range(len(masks) // 2):
        even = found[pl.ds(2 * pair, 1), :]
        odd = found[pl.ds(2 * pair + 1, 1), :]
        p = jnp.where(low, even, pltpu.roll(odd, ny // 2, 1))
        q = jnp.where(low, pltpu.roll(even, ny // 2, 1), odd)
        turns = (x * p.astype(jnp.int32)) & (nx - 1)
        angle = turns.astype(F32) * (2.0 * math.pi / nx)
        for k, values in enumerate((jnp.cos(angle), -jnp.sin(angle))):
            high = values.astype(jnp.bfloat16)
            rest = (values - high.astype(F32)).astype(jnp.bfloat16)
            for part, value in enumerate((high, high, rest)):
                table[pl.ds((2 * part + k) * nx, nx), pl.ds(pair * ny, ny)] = value
        qrow[:, pl.ds(pair * ny, ny)] = jnp.broadcast_to(q, (8, ny))
    for pair, found_now in enumerate(picks_of(direction, ytable, table, qrow)):
        picks[2 * pair : 2 * pair + 2, :] = jnp.concatenate(found_now, axis=0)


def picks_of(field, ytable, table, qrow):
    nx, ny = field.shape[2:]
    plane = field[:, PLANES - 1].reshape(2 * nx, ny)
    m = lax.dot_general(
        ytable[...],
        plane,
        (((1,), (1,)), ((), ())),
        precision=lax.Precision.HIGHEST,
        preferred_element_type=F32,
    )
    sign = jnp.where(lanes((nx, ny)) < ny // 2, -1.0, 1.0)
    t = m[:nx] + sign * pltpu.roll(m[nx:], nx, 1)
    both = jnp.concatenate([-sign * t, pltpu.roll(t, nx, 1)], axis=0) * (1.0 / math.sqrt(nx * ny))
    high = both.astype(jnp.bfloat16)
    rest = (both - high.astype(F32)).astype(jnp.bfloat16)
    spectrum = jnp.dot(jnp.concatenate([high, rest, high], axis=1), table[...], preferred_element_type=F32)
    at_row = lax.broadcasted_iota(jnp.int32, (nx, ny), 0).astype(F32) - ORD_HALF
    result = []
    for pair in range(qrow.shape[1] // ny):
        columns = slice(pair * ny, (pair + 1) * ny)
        chosen = at_row == qrow[0:1, columns]
        result.append(
            [
                jnp.sum(jnp.where(chosen, spectrum[k * nx : (k + 1) * nx, columns], 0.0), axis=0, keepdims=True)
                for k in range(2)
            ]
        )
    return result


def third_kernel(
    masks, layout, at, own, direction, image, smooth2, weight, w1r, w1i, w2r, w2i, ytable, xtable, qrow, picks, *refs
):
    n = max(i for i, _ in layout) + 1
    gathered, refs = refs[:n], refs[n:]
    (corrected, last_image, halfway, pay, alpha), refs = refs[:5], refs[5:]
    u, v, tmp, ec = refs[:4]
    coarse = refs[4:]
    me, zero = at[0], at[2]
    pieces = [(gathered[i], j) for i, j in layout]
    nx, ny = own.shape[2:]
    half = nx // 2
    coarse_solve(me, zero, masks, pieces, 2, w1r, w1i, w2r, w2i, *coarse, ec)
    add_correction(ec, smooth2, v, tmp, 6, nx)

    def sweep(src, dst, p, r0, rows):
        sr, si = around(src, p, r0, zero)
        wr, wi = weight[0, p + OUTER, rows], weight[1, p + OUTER, rows]
        vr, vi = cmul(wr, wi, image[0, p, rows] + sr, image[1, p, rows] + si)
        put(dst, 0, p, r0, KEEP * mid(src, 0, p, r0) + vr, nx)
        put(dst, 1, p, r0, KEEP * mid(src, 1, p, r0) + vi, nx)

    planes_of(2, 10, nx, lambda *a: sweep(v, u, *a))
    planes_of(3, 9, nx, lambda *a: sweep(u, v, *a))

    sums = 0.0
    for i, j in layout:
        sums = sums + gathered[i][j, pl.ds(2 * half, 8), :]
    rho, cr, ci = [jnp.sum(sums[k : k + 1], axis=1, keepdims=True) for k in range(3)]
    modulus = cr * cr + ci * ci
    ar = rho * cr / modulus
    ai = -rho * ci / modulus
    dots = [0.0, 0.0, 0.0]
    for q in range(PLANES):
        for r0 in range(0, nx, CHUNK):
            rows = pl.ds(r0, CHUNK)
            p = 4 + q
            sr, si = around(v, p, r0, zero)
            hr, hi = helm_of(own[2, q, rows])
            wr, wi = mid(v, 0, p, r0), mid(v, 1, p, r0)
            br, bi = cmul(hr, hi, wr, wi)
            br, bi = br + 6.0 * wr - sr, bi + 6.0 * wi - si
            ir, ii = image[0, p, rows], image[1, p, rows]
            br, bi = cmul(ar, ai, br, bi)
            lr, li = ir - br, ii - bi
            tr, ti = cmul(ar, ai, ir, ii)
            hr, hi = own[0, q, rows] - tr, own[1, q, rows] - ti
            xr, xi = cmul(ar, ai, wr, wi)
            corrected[0, q, rows], corrected[1, q, rows] = direction[0, q, rows] - xr, direction[1, q, rows] - xi
            last_image[0, q, rows], last_image[1, q, rows] = lr, li
            halfway[0, q, rows], halfway[1, q, rows] = hr, hi
            dots[0] = dots[0] + lr * hr + li * hi
            dots[1] = dots[1] + lr * hi - li * hr
            dots[2] = dots[2] + lr * lr + li * li
    dots = [jnp.sum(t, axis=0, keepdims=True) for t in dots]
    row = lax.broadcasted_iota(jnp.int32, (8, ny), 0)
    alpha[...] = jnp.where(row == 0, ar, ai)

    for pair, found in enumerate(picks_of(corrected, ytable, xtable, qrow)):
        block = 0.0
        lines = [picks[2 * pair : 2 * pair + 1], picks[2 * pair + 1 : 2 * pair + 2]] + found + dots
        for k, line in enumerate(lines):
            block = jnp.where(row == k, line, block)
        pay[2 * pair] = block
        pay[2 * pair + 1] = block


def last_kernel(at, direction, corrected, last_image, halfway, alpha, got, solution, residual, pupil):
    group = got.shape[0]
    nx, ny = direction.shape[2:]
    total = got[0]
    for k in range(1, group):
        total = total + got[k]
    along_r, along_i, norm = [jnp.sum(total[k : k + 1], axis=1, keepdims=True) for k in (4, 5, 6)]
    wr = along_r / norm
    wi = along_i / norm
    ar = alpha[0:1, 0:1]
    ai = alpha[1:2, 0:1]
    for q in range(PLANES):
        for r0 in range(0, nx, CHUNK):
            rows = pl.ds(r0, CHUNK)
            xr, xi = cmul(ar, ai, direction[0, q, rows], direction[1, q, rows])
            yr, yi = cmul(wr, wi, corrected[0, q, rows], corrected[1, q, rows])
            solution[0, q, rows], solution[1, q, rows] = xr + yr, xi + yi
            zr, zi = cmul(wr, wi, last_image[0, q, rows], last_image[1, q, rows])
            residual[0, q, rows], residual[1, q, rows] = halfway[0, q, rows] - zr, halfway[1, q, rows] - zi
    tip = got[group - 1]
    xr, xi = cmul(ar, ai, tip[0:1], tip[1:2])
    yr, yi = cmul(wr, wi, tip[2:3], tip[3:4])
    both = jnp.concatenate([xr + yr, xi + yi] * 4, axis=0)
    both = jnp.where(at[1] == 1, pltpu.roll(both, ny // 2, 1), both)
    pupil[...] = both[:2, : ny // 2]


def exchange(x, mask, group):
    return lax.ppermute(x, "gz", [(i, i ^ mask) for i in range(group)])


def swap_across(x, group):
    pairs = []
    for i in range(1, group - 1, 2):
        pairs += [(i, i + 1), (i + 1, i)]
    return lax.ppermute(x, "gz", pairs)


def skip_across(x, group):
    pairs = []
    for i in range(group):
        target = i + 2 if i % 2 == 0 else i - 2
        if 0 <= target < group:
            pairs.append((i, target))
    return lax.ppermute(x, "gz", pairs)


def stages_of(group):
    stages = [[1]]
    stride = 2
    left = group // 2
    if left.bit_length() % 2 == 0:
        stages.insert(0, [stride])
        stride, left = 2 * stride, left // 2
    while left > 1:
        stages.insert(0, [stride, 2 * stride, 3 * stride])
        stride, left = 4 * stride, left // 4
    return stages


def gather(x, group):
    have, masks = x[None], [0]
    stages = stages_of(group)
    for masks_now in stages[:-1]:
        got = [exchange(have, m, group) for m in masks_now]
        masks = masks + [k ^ m for m in masks_now for k in masks]
        have = jnp.concatenate([have] + got, axis=0)
    (m,) = stages[-1]
    other = exchange(have, m, group)
    count = len(masks)
    layout = [(0, j) for j in range(count)] + [(1, j) for j in range(count)]
    return [have, other], masks + [k ^ m for k in masks], layout


def y_phases(nx, ny):
    q = np.arange(nx) - ORD_HALF
    turns = (q[:, None] * np.arange(ny)[None, :]) % ny
    angle = turns.astype(np.float64) * (2.0 * np.pi / ny)
    return np.concatenate([np.cos(angle), -np.sin(angle)], axis=0).astype(np.float32)


def on_device(source_term, material, orders):
    group = lax.axis_size("gz")
    _, planes, nx, ny = source_term.shape
    assert planes == PLANES and 2 * nx == ny and 2 * orders.shape[1] == ny
    me = lax.axis_index("gz")
    at = jnp.stack([me, me % 2, me * 0]).astype(jnp.int32)
    half = nx // 2

    fine = (2, PLANES, nx, ny)
    half_block = (3, OUTER, nx, ny)
    own, inner, outer = call(
        pack_kernel, [(3, PLANES, nx, ny), half_block, half_block], [at, source_term, material], []
    )
    swap = swap_across(inner, group)
    near = exchange(own, 1, group)
    swap_outer = swap_across(outer, group)
    skip = skip_across(outer, group)
    far = exchange(swap, 1, group)
    tall = nx + 2 * HALO
    (pay0,) = call(static_kernel, [(2 * half + half // 2 + 8, ny)], [at, own, orders], [(2, 2, nx, ny), (half, ny)])
    (pay1,) = call(
        first_kernel,
        [(4 * half + half // 2 + 8, ny)],
        [at, own, near, swap, pay0],
        [(2, 8, tall, ny), fine, (2, 8, tall, ny), (2, 2, nx, ny)],
    )
    gathered1, masks, layout = gather(pay1, group)
    window = (2, WINDOW, nx, ny)
    haloed = (2, WINDOW, tall, ny)
    shapes1 = (2 * group + 2 * PAD1, half, ny)
    shapes2 = (group + 2 * PAD2, half // 2, ny)
    f, weight, before, code = call(
        ahead_kernel, [window, window, haloed, (WINDOW, nx, ny)], [at, own, near, swap, swap_outer, skip, far], [haloed]
    )
    edge = (2, 2, nx, ny)
    direction, image, to_near, to_swap, pay2, w1r, w1i, w2r, w2i = call(
        functools.partial(second_kernel, masks, layout),
        [
            fine,
            (2, WINDOW - 8, nx, ny),
            edge,
            edge,
            (2 * half + 8, ny),
            shapes1,
            shapes1,
            shapes2,
            shapes2,
        ],
        [at, f, weight, before, code, *gathered1],
        [haloed, haloed, haloed, (2, 2, nx, ny), (WINDOW // 2, half, ny), window] + coarse_shapes(group, nx, ny),
    )
    near2 = exchange(to_near, 1, group)
    swap2 = swap_across(to_swap, group)
    wide, smooth2 = call(
        widen_kernel, [(2, 12, nx, ny), (2, 12, tall, ny)], [at, image, near2, swap2, weight], [(2, 12, tall, ny)]
    )
    ytable = jnp.asarray(y_phases(nx, ny))
    wanted = group * ny // 2
    xtable, qrow, picks = pl.pallas_call(
        functools.partial(phase_kernel, masks, layout, 4 * half + half // 2),
        out_shape=[
            jax.ShapeDtypeStruct((6 * nx, wanted), jnp.bfloat16),
            full((8, wanted)),
            full((group, ny)),
        ],
        in_specs=[SM] + [VM] * (2 + len(gathered1)),
        out_specs=[VM] * 3,
        scratch_shapes=[pltpu.VMEM((group, ny), F32)],
        compiler_params=pltpu.CompilerParams(vmem_limit_bytes=VMEM_LIMIT),
        cost_estimate=pl.CostEstimate(flops=4000000, bytes_accessed=600000, transcendentals=0),
        name="phases",
    )(at, ytable, direction, *gathered1)
    gathered2, masks, layout = gather(pay2, group)
    corrected, last_image, halfway, pay3, alpha = call(
        functools.partial(third_kernel, masks, layout),
        [fine, fine, fine, (group, 8, ny), (8, ny)],
        [
            at,
            own,
            direction,
            wide,
            smooth2,
            weight,
            w1r,
            w1i,
            w2r,
            w2i,
            ytable,
            xtable,
            qrow,
            picks,
            *gathered2,
        ],
        [(2, 12, tall, ny), (2, 12, tall, ny), (2, 2, nx, ny), (6, half, ny)] + coarse_shapes(group, nx, ny),
    )
    got = lax.all_to_all(pay3, "gz", 0, 0)
    solution, residual, pupil = call(
        last_kernel, [fine, fine, (2, ny // 2)], [at, direction, corrected, last_image, halfway, alpha, got], []
    )
    return solution, residual, pupil


def solution(mesh):
    return jax.shard_map(
        on_device,
        mesh=mesh,
        in_specs=(
            P(None, ("clip", "gz"), None, None),
            P(("clip", "gz"), None, None),
            P(None, "gz"),
        ),
        out_specs=(
            P(None, ("clip", "gz"), None, None),
            P(None, ("clip", "gz"), None, None),
            P(None, ("clip", "gz")),
        ),
        check_vma=False,
    )
```

```python
import functools
import math

import jax
import jax.numpy as jnp
import numpy as np
from jax import lax
from jax.experimental import pallas as pl
from jax.experimental.pallas import tpu as pltpu
from jax.sharding import PartitionSpec as P


ORD_HALF = 22
HELM_TABLE = ((-0.5, 0.0), (1.0, -1.4), (-1.2, 0.0))
SHIFT_TABLE = ((-0.5, -0.25), (1.0, -0.25 * math.sqrt(11.84)), (-1.2, -0.6))
RELAX = 0.8
KEEP = 1.0 - RELAX
PLANES = 4
OUTER = 2
OWN = PLANES + OUTER
WINDOW = PLANES + 2 * OWN
PAD1 = 8
PAD2 = 4
H1 = 0.25
H2 = 0.0625
F32 = jnp.float32
VMEM_LIMIT = 28 * 2**20

WEIGHTS = tuple(RELAX / complex(6.0 + s[0], s[1]) for s in SHIFT_TABLE)


def pick(code, values):
    return jnp.where(
        code == 1.0,
        values[0],
        jnp.where(code == 2.0, values[1], jnp.where(code == 3.0, values[2], 0.0)),
    )


def weight_of(code):
    return pick(code, [w.real for w in WEIGHTS]), pick(code, [w.imag for w in WEIGHTS])


def shift_of(code):
    return pick(code, [s[0] for s in SHIFT_TABLE]), pick(code, [s[1] for s in SHIFT_TABLE])


def helm_of(code):
    return pick(code, [s[0] for s in HELM_TABLE]), pick(code, [s[1] for s in HELM_TABLE])


def cmul(ar, ai, br, bi):
    return ar * br - ai * bi, ar * bi + ai * br


HALO = 8
CHUNK = 16


def put(ref, c, p, r0, value, nx):
    n = value.shape[0]
    ref[c, p, pl.ds(HALO + r0, n), :] = value
    if r0 == 0:
        ref[c, p, pl.ds(HALO + nx, 1), :] = value[:1]
    if r0 + n == nx:
        ref[c, p, pl.ds(HALO - 1, 1), :] = value[n - 1 :]


def mid(ref, c, p, r0, n=CHUNK):
    return ref[c, p, pl.ds(HALO + r0, n), :]


def around(ref, p, r0, zero):
    sums = []
    for c in range(2):
        m = mid(ref, c, p, r0)
        ny = m.shape[1]
        total = mid(ref, c, p - 1, r0) + mid(ref, c, p + 1, r0)
        total = total + ref[c, p, pl.ds(HALO - 1 + r0 + zero, CHUNK), :]
        total = total + ref[c, p, pl.ds(HALO + 1 + r0 + zero, CHUNK), :]
        total = total + pltpu.roll(m, 1, 1) + pltpu.roll(m, ny - 1, 1)
        sums.append(total)
    return sums


def planes_of(lower, upper, nx, body, most=4):
    size = max(n for n in range(1, most + 1) if (upper - lower) % n == 0)

    def step(k, carry):
        for j in range(size):
            for r0 in range(0, nx, CHUNK):
                body(lower + k * size + j, r0, pl.ds(r0, CHUNK))
        return carry

    lax.fori_loop(0, (upper - lower) // size, step, 0)


def lanes(shape):
    return lax.broadcasted_iota(jnp.int32, shape, len(shape) - 1)


def put_packed(ref, p, count, value):
    n = value.shape[1]
    ref[pl.ds(p, count), pl.ds(HALO, n), :] = value
    ref[pl.ds(p, count), pl.ds(HALO + n, 1), :] = value[:, :1]
    ref[pl.ds(p, count), pl.ds(HALO - 1, 1), :] = value[:, n - 1 :]


def mid_packed(ref, p, count):
    return ref[pl.ds(p, count), pl.ds(HALO, ref.shape[1] - 2 * HALO), :]


def around_packed(ref, p, count, part, zero):
    m = mid_packed(ref, p, count)
    n, width = m.shape[1:]
    total = mid_packed(ref, p - 1, count) + mid_packed(ref, p + 1, count)
    total = total + ref[pl.ds(p, count), pl.ds(HALO - 1 + zero, n), :]
    total = total + ref[pl.ds(p, count), pl.ds(HALO + 1 + zero, n), :]
    at = lanes((1, 1, width)) % part
    before = jnp.where(at == 0, pltpu.roll(m, width + 1 - part, 2), pltpu.roll(m, 1, 2))
    after = jnp.where(at == part - 1, pltpu.roll(m, part - 1, 2), pltpu.roll(m, width - 1, 2))
    return total + before + after


def cmul_packed(wr, wi, g, part):
    return wr * g + wi * pltpu.roll(g, part, g.ndim - 1)


def weights_packed(shift, part, factor):
    other = pltpu.roll(shift, part, 1)
    real_lane = lanes(shift.shape) % (2 * part) < part
    dr = 6.0 * factor + jnp.where(real_lane, shift, other)
    di = jnp.where(real_lane, other, shift)
    scale = RELAX / (dr * dr + di * di)
    return jnp.where(real_lane, dr, -di) * scale


def dot_exact(a, b):
    high = a.astype(jnp.bfloat16)
    low = (a - high.astype(F32)).astype(jnp.bfloat16)
    b = b.astype(jnp.bfloat16)
    both = jnp.concatenate([high, low], axis=1)
    return jnp.dot(both, jnp.concatenate([b, b], axis=0), preferred_element_type=F32)


def iota2(rows, cols):
    return (
        lax.broadcasted_iota(jnp.int32, (rows, cols), 0),
        lax.broadcasted_iota(jnp.int32, (rows, cols), 1),
    )


def restrict_fine(tmp):
    nx, ny = tmp.shape[1:]
    half = nx // 2
    rows = [tmp[c, pl.ds(0, half, stride=2), :] + tmp[c, pl.ds(1, half, stride=2), :] for c in range(2)]
    r, c = iota2(2 * ny, ny)
    pool = jnp.where(r // 2 == c, 0.125, 0.0).astype(F32)
    return dot_exact(jnp.concatenate(rows, axis=1), pool)


def pool_level1(ny):
    r, c = iota2(ny, ny)
    return jnp.where(r // 2 == c % (ny // 2), 0.125, 0.0).astype(F32)


def full(shape_dtype):
    return jax.ShapeDtypeStruct(shape_dtype, F32)


VM = pl.BlockSpec(memory_space=pltpu.VMEM)
SM = pl.BlockSpec(memory_space=pltpu.SMEM)


def call(body, outs, inputs, scratch):
    size = sum(4 * math.prod(x.shape) for x in inputs) + sum(4 * math.prod(o) for o in outs)
    return pl.pallas_call(
        body,
        out_shape=[full(o) for o in outs],
        in_specs=[SM] + [VM] * (len(inputs) - 1),
        out_specs=[VM] * len(outs),
        scratch_shapes=[pltpu.VMEM(s, F32) for s in scratch],
        compiler_params=pltpu.CompilerParams(vmem_limit_bytes=VMEM_LIMIT),
        cost_estimate=pl.CostEstimate(flops=40 * size, bytes_accessed=size, transcendentals=0),
    )(*inputs)


def pack_kernel(at, source, material, own, inner, outer):
    odd = at[1]
    nx = source.shape[2]

    def join(p, r0, rows):
        for c in range(2):
            own[c, p, rows] = source[c, p, rows]
        own[2, p, rows] = (material[p, rows] + 1).astype(F32)

    planes_of(0, PLANES, nx, join)

    def halves(p, r0, rows):
        for c in range(3):
            inner[c, p, rows] = own[c, p + OUTER * odd, rows]
            outer[c, p, rows] = own[c, p + OUTER * (1 - odd), rows]

    planes_of(0, OUTER, nx, halves)


def first_kernel(at, own, near, swap, static, out, u, e1, u2, tmp):
    odd, zero = at[1], at[2]
    nx, _ = own.shape[2:]

    def fill(block, lower, upper, first):
        def body(p, r0, rows):
            wr, wi = weight_of(block[2, p, rows])
            ur, ui = cmul(wr, wi, block[0, p, rows], block[1, p, rows])
            put(u, 0, first + p, r0, ur, nx)
            put(u, 1, first + p, r0, ui, nx)

        planes_of(lower, upper, nx, body)

    fill(own, 0, PLANES, 2)

    @pl.when(odd == 0)
    def _():
        fill(swap, 0, 2, 0)
        fill(near, 0, 2, 6)

    @pl.when(odd == 1)
    def _():
        fill(near, 2, 4, -2)
        fill(swap, 0, 2, 6)

    def smooth(p, block, q, r0, rows):
        sr, si = around(u, p, r0, zero)
        er = KEEP * block[0, q, rows] + sr
        ei = KEEP * block[1, q, rows] + si
        wr, wi = weight_of(block[2, q, rows])
        vr, vi = cmul(wr, wi, er, ei)
        put(u2, 0, p, r0, vr, nx)
        put(u2, 1, p, r0, vi, nx)
        return er, ei

    def inner(q, r0, rows):
        er, ei = smooth(2 + q, own, q, r0, rows)
        e1[0, q, rows] = er
        e1[1, q, rows] = ei

    planes_of(0, PLANES, nx, inner)

    def outer(block, q, p):
        planes_of(q, q + 1, nx, lambda q, r0, rows: smooth(p, block, q, r0, rows))

    @pl.when(odd == 0)
    def _():
        outer(swap, OUTER - 1, 1)
        outer(near, 0, 6)

    @pl.when(odd == 1)
    def _():
        outer(near, PLANES - 1, 1)
        outer(swap, 0, 6)

    half = nx // 2
    for q in range(PLANES // 2):
        for r0 in range(0, nx, CHUNK):
            rows = pl.ds(r0, CHUNK)
            total = [0.0, 0.0]
            for p in (2 * q, 2 * q + 1):
                s = around(u2, 2 + p, r0, zero)
                for c in range(2):
                    total[c] = total[c] + KEEP * e1[c, p, rows] + s[c]
            for c in range(2):
                tmp[q, c, rows] = total[c]
        out[pl.ds(half * q, half), :] = restrict_fine(tmp.at[q])
    out[pl.ds(2 * half, static.shape[0]), :] = static[...]


def static_kernel(at, own, orders, out, tmp, tmp1):
    nx, ny = own.shape[2:]
    half = nx // 2
    planes = []
    for q in range(PLANES // 2):
        for r0 in range(0, nx, CHUNK):
            rows = pl.ds(r0, CHUNK)
            below, above = shift_of(own[2, 2 * q, rows]), shift_of(own[2, 2 * q + 1, rows])
            for c in range(2):
                tmp[q, c, rows] = below[c] + above[c]
        shift = restrict_fine(tmp.at[q])
        out[pl.ds(half * q, half), :] = weights_packed(shift, ny // 2, H1)
        planes.append(shift)
    tmp1[...] = planes[0] + planes[1]
    pooled = tmp1[pl.ds(0, half // 2, stride=2), :] + tmp1[pl.ds(1, half // 2, stride=2), :]
    shift2 = dot_exact(pooled, pool_level1(ny))
    out[pl.ds(2 * half, half // 2), :] = weights_packed(shift2, ny // 4, H2)
    wanted = orders[...].astype(F32)
    line = jnp.concatenate([wanted[0:1], wanted[1:2]], axis=1)
    out[pl.ds(2 * half + half // 2, 8), :] = jnp.broadcast_to(line, (8, ny))


def coarse_shapes(group, nx, ny):
    n1 = (2 * group + 2 * PAD1, nx // 2 + 2 * HALO, ny)
    n2 = (group + 2 * PAD2, nx // 4 + 2 * HALO, ny)
    return [n1[:1] + (nx // 2, ny), n1, n1, n1, n1, n2[:1] + (nx // 4, ny), n2, n2, (nx // 2, ny), (group * (nx // 2), ny)]


def clear_edges(ref, pad, count):
    zero = jnp.zeros(ref.shape[1:], F32)
    top = ref.shape[0] - pad
    for k in range(count):
        ref[pad - 1 - k] = zero
        ref[top + k] = zero


def coarse_weights(me, masks, pieces, w1r, w1i, w2r, w2i):
    half, ny = w1r.shape[1:]
    quarter = half // 2
    for ref, pad in ((w1r, PAD1), (w1i, PAD1), (w2r, PAD2), (w2i, PAD2)):
        clear_edges(ref, pad, pad - 1)

    def expand(w, part):
        other = pltpu.roll(w, part, 1)
        real_lane = lanes(w.shape) % (2 * part) < part
        return jnp.where(real_lane, w, other), jnp.where(real_lane, -other, w)

    for mask, (piece, j) in zip(masks, pieces, strict=True):
        d = me ^ mask
        for k in range(2):
            wr, wi = expand(piece[j, pl.ds(half * (2 + k), half), :], ny // 2)
            w1r[PAD1 + 2 * d + k] = wr
            w1i[PAD1 + 2 * d + k] = wi
        wr, wi = expand(piece[j, pl.ds(4 * half, quarter), :], ny // 4)
        w2r[PAD2 + d] = wr
        w2i[PAD2 + d] = wi


def chunked(lower, count, most, body):
    size = max(n for n in range(1, most + 1) if count % n == 0)

    def step(k, carry):
        body(lower + k * size, size)
        return carry

    lax.fori_loop(0, count // size, step, 0)


def coarse_solve(me, zero, masks, pieces, reach, w1r, w1i, w2r, w2i, g1, u1, u2, v1, e1, g2, va, vb, tmp, pool, out):
    half, ny = tmp.shape
    quarter = half // 2
    group = len(masks)
    part1, part2 = ny // 2, ny // 4
    n1 = 2 * group
    clear_edges(g1, PAD1, reach + 1)
    clear_edges(u1, PAD1, 1)
    clear_edges(u2, PAD1, 1)
    clear_edges(v1, PAD1, reach + 2)
    clear_edges(va, PAD2, 1)
    clear_edges(vb, PAD2, PAD2 - 1)
    for mask, (piece, j) in zip(masks, pieces, strict=True):
        p = PAD1 + 2 * (me ^ mask)
        g = piece[j, pl.ds(0, 2 * half), :].reshape(2, half, ny)
        g1[pl.ds(p, 2)] = g
        put_packed(u1, p, 2, cmul_packed(w1r[pl.ds(p, 2)], w1i[pl.ds(p, 2)], g, part1))

    def pre(p, n):
        e = KEEP * g1[pl.ds(p, n)] + H1 * around_packed(u1, p, n, part1, zero)
        u = cmul_packed(w1r[pl.ds(p, n)], w1i[pl.ds(p, n)], e, part1)
        e1[pl.ds(p, n), pl.ds(0, half), :] = e
        put_packed(u2, p, n, u)
        put_packed(v1, p, n, mid_packed(u1, p, n) + u)

    chunked(PAD1, n1, 16, pre)

    def coarser(p, n):
        e = KEEP * e1[pl.ds(p, n), pl.ds(0, half), :] + H1 * around_packed(u2, p, n, part1, zero)
        e = e.reshape(n // 2, 2, half, ny)
        pairs = (e[:, 0] + e[:, 1]).reshape(n // 2 * half, ny)
        pool[pl.ds((p - PAD1) // 2 * half, n // 2 * half), :] = pairs

    chunked(PAD1, n1, 16, coarser)
    rows = group * quarter
    flat = pool[pl.ds(0, rows, stride=2), :] + pool[pl.ds(1, rows, stride=2), :]
    r2 = dot_exact(flat, pool_level1(ny)).reshape(group, quarter, ny)
    inside = pl.ds(PAD2, group)
    g2[inside] = r2
    put_packed(va, PAD2, group, cmul_packed(w2r[inside], w2i[inside], r2, part2))
    for src, dst in ((va, vb), (vb, va), (va, vb)):

        def sweep(p, n, src=src, dst=dst):
            s = g2[pl.ds(p, n)] + H2 * around_packed(src, p, n, part2, zero)
            v = KEEP * mid_packed(src, p, n) + cmul_packed(w2r[pl.ds(p, n)], w2i[pl.ds(p, n)], s, part2)
            put_packed(dst, p, n, v)

        chunked(PAD2, group, 16, sweep)
    reach2 = (reach + 3) // 2
    count = 2 * reach2 + 1
    flat = mid_packed(vb, PAD2 + me - reach2, count).reshape(count * quarter, ny)
    r, c = iota2(ny, ny)
    spread = jnp.where(c // 2 == r, 1.0, 0.0).astype(F32)
    e2 = dot_exact(flat, spread)
    pool[pl.ds(0, count * quarter, stride=2), :] = e2
    pool[pl.ds(1, count * quarter, stride=2), :] = e2
    base = PAD1 + 2 * (me - reach2)
    for k in range(count):
        add = pool[pl.ds(k * half, half), :]
        both = mid_packed(v1, base + 2 * k, 2) + add[None]
        put_packed(v1, base + 2 * k, 2, both)

    def post(src, p, n):
        s = g1[pl.ds(p, n)] + H1 * around_packed(src, p, n, part1, zero)
        return KEEP * mid_packed(src, p, n) + cmul_packed(w1r[pl.ds(p, n)], w1i[pl.ds(p, n)], s, part1)

    start = PAD1 + 2 * me

    def third(p, n):
        put_packed(u1, p, n, post(v1, p, n))

    def fourth(p, n):
        out[pl.ds(p - (start - reach), n)] = post(u1, p, n)

    chunked(start - reach - 1, 2 * reach + 4, 10, third)
    chunked(start - reach, 2 * reach + 2, 8, fourth)


def add_correction(ec, before, v, tmp, planes, nx):
    half, ny = ec.shape[1:]
    r, c = iota2(ny, 2 * ny)
    spread = jnp.where(c // 2 == r, 1.0, 0.0).astype(F32)

    def body(m, carry):
        k = 2 * m
        both = dot_exact(ec[pl.ds(k, 2)].reshape(2 * half, ny), spread)
        for j in range(2):
            for c in range(2):
                e = both[j * half : (j + 1) * half, c * ny : (c + 1) * ny]
                tmp[j, c, pl.ds(0, half, stride=2), :] = e
                tmp[j, c, pl.ds(1, half, stride=2), :] = e
        for j in range(2):
            for c in range(2):
                for r0 in range(0, nx, CHUNK):
                    add = tmp[j, c, pl.ds(r0, CHUNK)]
                    for p in (2 * (k + j), 2 * (k + j) + 1):
                        put(v, c, p, r0, mid(before, c, p, r0) + add, nx)
        return carry

    lax.fori_loop(0, planes // 2, body, 0)


def ahead_kernel(at, own, near, swap, swap_outer, skip, far, f, weight, v, code, u):
    odd, zero = at[1], at[2]
    nx = own.shape[2]

    def fill(block, first):
        def body(q, r0, rows):
            p = first + q
            c = block[2, q, rows]
            wr, wi = weight_of(c)
            fr, fi = block[0, q, rows], block[1, q, rows]
            ur, ui = cmul(wr, wi, fr, fi)
            f[0, p, rows], f[1, p, rows] = fr, fi
            weight[0, p, rows], weight[1, p, rows] = wr, wi
            put(u, 0, p, r0, ur, nx)
            put(u, 1, p, r0, ui, nx)
            code[p, rows] = c

        planes_of(0, block.shape[1], nx, body)

    top = OWN + PLANES
    fill(own, OWN)
    fill(near, top - 2 * PLANES * odd)
    fill(swap, PLANES + 3 * OUTER * odd)
    fill(swap_outer, OUTER + 5 * OUTER * odd)
    fill(skip, (WINDOW - OUTER) * odd)
    fill(far, (WINDOW - OUTER) * (1 - odd))

    def pre(p, r0, rows):
        sr, si = around(u, p, r0, zero)
        er = KEEP * f[0, p, rows] + sr
        ei = KEEP * f[1, p, rows] + si
        vr, vi = cmul(weight[0, p, rows], weight[1, p, rows], er, ei)
        put(v, 0, p, r0, mid(u, 0, p, r0) + vr, nx)
        put(v, 1, p, r0, mid(u, 1, p, r0) + vi, nx)

    planes_of(1, WINDOW - 1, nx, pre, 7)


def second_kernel(masks, layout, at, f, weight, before, code, *refs):
    n = max(i for i, _ in layout) + 1
    gathered, refs = refs[:n], refs[n:]
    (direction, image, to_near, to_swap, pay, w1r, w1i, w2r, w2i), refs = refs[:9], refs[9:]
    u, u2, v, tmp, ec, e1 = refs[:6]
    coarse = refs[6:]
    me, odd, zero = at[0], at[1], at[2]
    nx, ny = f.shape[2:]
    pieces = [(gathered[i], j) for i, j in layout]
    coarse_weights(me, masks, pieces, w1r, w1i, w2r, w2i)
    coarse_solve(me, zero, masks, pieces, OWN // 2, w1r, w1i, w2r, w2i, *coarse, ec)
    add_correction(ec, before, v, tmp, WINDOW // 2, nx)

    def sweep(src, dst, p, r0, rows):
        sr, si = around(src, p, r0, zero)
        vr, vi = cmul(weight[0, p, rows], weight[1, p, rows], f[0, p, rows] + sr, f[1, p, rows] + si)
        put(dst, 0, p, r0, KEEP * mid(src, 0, p, r0) + vr, nx)
        put(dst, 1, p, r0, KEEP * mid(src, 1, p, r0) + vi, nx)

    planes_of(2, WINDOW - 2, nx, lambda *a: sweep(v, u, *a), 6)
    planes_of(3, WINDOW - 3, nx, lambda *a: sweep(u, v, *a), 10)

    def apply(p, r0, rows):
        sr, si = around(v, p, r0, zero)
        c = code[p, rows]
        hr, hi = helm_of(c)
        vr, vi = mid(v, 0, p, r0), mid(v, 1, p, r0)
        ar, ai = cmul(hr, hi, vr, vi)
        ar = jnp.where(c > 0.0, ar + 6.0 * vr - sr, 0.0)
        ai = jnp.where(c > 0.0, ai + 6.0 * vi - si, 0.0)
        image[0, p - 4, rows] = ar
        image[1, p - 4, rows] = ai
        ur, ui = cmul(weight[0, p, rows], weight[1, p, rows], ar, ai)
        put(u, 0, p, r0, ur, nx)
        put(u, 1, p, r0, ui, nx)

    planes_of(4, WINDOW - 4, nx, apply, 8)
    rho, cross_r, cross_i = 0.0, 0.0, 0.0
    for q in range(PLANES):
        for r0 in range(0, nx, CHUNK):
            rows = pl.ds(r0, CHUNK)
            fr, fi = f[0, OWN + q, rows], f[1, OWN + q, rows]
            ir, ii = image[0, OWN - 4 + q, rows], image[1, OWN - 4 + q, rows]
            rho = rho + fr * fr + fi * fi
            cross_r = cross_r + fr * ir + fi * ii
            cross_i = cross_i + fr * ii - fi * ir
            for c in range(2):
                direction[c, q, rows] = mid(v, c, OWN + q, r0)
    half = nx // 2
    row = lax.broadcasted_iota(jnp.int32, (8, ny), 0)
    sums = [jnp.sum(t, axis=0, keepdims=True) for t in (rho, cross_r, cross_i)]
    tail = jnp.where(row == 0, sums[0], jnp.where(row == 1, sums[1], jnp.where(row == 2, sums[2], 0.0)))
    pay[pl.ds(2 * half, 8), :] = tail

    def edges(q, r0, rows):
        for c in range(2):
            to_near[c, q, rows] = image[c, OWN - 4 + q + 2 * odd, rows]
            to_swap[c, q, rows] = image[c, OWN - 2 + q - 2 * odd, rows]

    planes_of(0, 2, nx, edges)

    def pre2(p, r0, rows):
        sr, si = around(u, p, r0, zero)
        er = KEEP * image[0, p - 4, rows] + sr
        ei = KEEP * image[1, p - 4, rows] + si
        vr, vi = cmul(weight[0, p, rows], weight[1, p, rows], er, ei)
        e1[0, p, rows], e1[1, p, rows] = er, ei
        put(u2, 0, p, r0, vr, nx)
        put(u2, 1, p, r0, vi, nx)

    planes_of(OWN - 1, OWN + PLANES + 1, nx, pre2, 6)
    for q in range(PLANES // 2):
        for r0 in range(0, nx, CHUNK):
            rows = pl.ds(r0, CHUNK)
            total = [0.0, 0.0]
            for k in range(2):
                p = OWN + 2 * q + k
                s = around(u2, p, r0, zero)
                for c in range(2):
                    total[c] = total[c] + KEEP * e1[c, p, rows] + s[c]
            for c in range(2):
                tmp[q, c, rows] = total[c]
        pay[pl.ds(half * q, half), :] = restrict_fine(tmp.at[q])


def widen_kernel(at, image, near, swap, weight, wide, smooth, u):
    odd, zero = at[1], at[2]
    nx = image.shape[2]

    def fill(block, first):
        def body(q, r0, rows):
            p = first + q
            fr, fi = block[0, q, rows], block[1, q, rows]
            ur, ui = cmul(weight[0, p + OUTER, rows], weight[1, p + OUTER, rows], fr, fi)
            wide[0, p, rows], wide[1, p, rows] = fr, fi
            put(u, 0, p, r0, ur, nx)
            put(u, 1, p, r0, ui, nx)

        planes_of(0, block.shape[1], nx, body)

    fill(image, 2)
    fill(near, 10 - 10 * odd)
    fill(swap, 10 * odd)

    def pre(p, r0, rows):
        sr, si = around(u, p, r0, zero)
        er = KEEP * wide[0, p, rows] + sr
        ei = KEEP * wide[1, p, rows] + si
        vr, vi = cmul(weight[0, p + OUTER, rows], weight[1, p + OUTER, rows], er, ei)
        put(smooth, 0, p, r0, mid(u, 0, p, r0) + vr, nx)
        put(smooth, 1, p, r0, mid(u, 1, p, r0) + vi, nx)

    planes_of(1, 11, nx, pre, 5)


def phase_kernel(masks, layout, row, at, ytable, direction, *refs):
    n = max(i for i, _ in layout) + 1
    gathered = refs[:n]
    table, qrow, picks, found = refs[n:]
    me = at[0]
    ny = found.shape[1]
    nx = table.shape[0] // 6
    for mask, (i, j) in zip(masks, layout, strict=True):
        found[pl.ds(me ^ mask, 1), :] = gathered[i][j, pl.ds(row, 1), :]
    low = lanes((1, ny)) < ny // 2
    x = lax.broadcasted_iota(jnp.int32, (nx, ny), 0)
    for pair in range(len(masks) // 2):
        even = found[pl.ds(2 * pair, 1), :]
        odd = found[pl.ds(2 * pair + 1, 1), :]
        p = jnp.where(low, even, pltpu.roll(odd, ny // 2, 1))
        q = jnp.where(low, pltpu.roll(even, ny // 2, 1), odd)
        turns = (x * p.astype(jnp.int32)) & (nx - 1)
        angle = turns.astype(F32) * (2.0 * math.pi / nx)
        for k, values in enumerate((jnp.cos(angle), -jnp.sin(angle))):
            high = values.astype(jnp.bfloat16)
            rest = (values - high.astype(F32)).astype(jnp.bfloat16)
            for part, value in enumerate((high, high, rest)):
                table[pl.ds((2 * part + k) * nx, nx), pl.ds(pair * ny, ny)] = value
        qrow[:, pl.ds(pair * ny, ny)] = jnp.broadcast_to(q, (8, ny))
    for pair, found_now in enumerate(picks_of(direction, ytable, table, qrow)):
        picks[2 * pair : 2 * pair + 2, :] = jnp.concatenate(found_now, axis=0)


def picks_of(field, ytable, table, qrow):
    nx, ny = field.shape[2:]
    plane = field[:, PLANES - 1].reshape(2 * nx, ny)
    m = lax.dot_general(
        ytable[...],
        plane,
        (((1,), (1,)), ((), ())),
        precision=lax.Precision.HIGHEST,
        preferred_element_type=F32,
    )
    sign = jnp.where(lanes((nx, ny)) < ny // 2, -1.0, 1.0)
    t = m[:nx] + sign * pltpu.roll(m[nx:], nx, 1)
    both = jnp.concatenate([-sign * t, pltpu.roll(t, nx, 1)], axis=0) * (1.0 / math.sqrt(nx * ny))
    high = both.astype(jnp.bfloat16)
    rest = (both - high.astype(F32)).astype(jnp.bfloat16)
    spectrum = jnp.dot(jnp.concatenate([high, rest, high], axis=1), table[...], preferred_element_type=F32)
    at_row = lax.broadcasted_iota(jnp.int32, (nx, ny), 0).astype(F32) - ORD_HALF
    result = []
    for pair in range(qrow.shape[1] // ny):
        columns = slice(pair * ny, (pair + 1) * ny)
        chosen = at_row == qrow[0:1, columns]
        result.append(
            [
                jnp.sum(jnp.where(chosen, spectrum[k * nx : (k + 1) * nx, columns], 0.0), axis=0, keepdims=True)
                for k in range(2)
            ]
        )
    return result


def third_kernel(
    masks, layout, at, own, direction, image, smooth2, weight, w1r, w1i, w2r, w2i, ytable, xtable, qrow, picks, *refs
):
    n = max(i for i, _ in layout) + 1
    gathered, refs = refs[:n], refs[n:]
    (corrected, last_image, halfway, pay, alpha), refs = refs[:5], refs[5:]
    u, v, tmp, ec = refs[:4]
    coarse = refs[4:]
    me, zero = at[0], at[2]
    pieces = [(gathered[i], j) for i, j in layout]
    nx, ny = own.shape[2:]
    half = nx // 2
    coarse_solve(me, zero, masks, pieces, 2, w1r, w1i, w2r, w2i, *coarse, ec)
    add_correction(ec, smooth2, v, tmp, 6, nx)

    def sweep(src, dst, p, r0, rows):
        sr, si = around(src, p, r0, zero)
        wr, wi = weight[0, p + OUTER, rows], weight[1, p + OUTER, rows]
        vr, vi = cmul(wr, wi, image[0, p, rows] + sr, image[1, p, rows] + si)
        put(dst, 0, p, r0, KEEP * mid(src, 0, p, r0) + vr, nx)
        put(dst, 1, p, r0, KEEP * mid(src, 1, p, r0) + vi, nx)

    planes_of(2, 10, nx, lambda *a: sweep(v, u, *a), 8)
    planes_of(3, 9, nx, lambda *a: sweep(u, v, *a), 6)

    sums = 0.0
    for i, j in layout:
        sums = sums + gathered[i][j, pl.ds(2 * half, 8), :]
    rho, cr, ci = [jnp.sum(sums[k : k + 1], axis=1, keepdims=True) for k in range(3)]
    modulus = cr * cr + ci * ci
    ar = rho * cr / modulus
    ai = -rho * ci / modulus
    dots = [0.0, 0.0, 0.0]
    for q in range(PLANES):
        for r0 in range(0, nx, CHUNK):
            rows = pl.ds(r0, CHUNK)
            p = 4 + q
            sr, si = around(v, p, r0, zero)
            hr, hi = helm_of(own[2, q, rows])
            wr, wi = mid(v, 0, p, r0), mid(v, 1, p, r0)
            br, bi = cmul(hr, hi, wr, wi)
            br, bi = br + 6.0 * wr - sr, bi + 6.0 * wi - si
            ir, ii = image[0, p, rows], image[1, p, rows]
            br, bi = cmul(ar, ai, br, bi)
            lr, li = ir - br, ii - bi
            tr, ti = cmul(ar, ai, ir, ii)
            hr, hi = own[0, q, rows] - tr, own[1, q, rows] - ti
            xr, xi = cmul(ar, ai, wr, wi)
            corrected[0, q, rows], corrected[1, q, rows] = direction[0, q, rows] - xr, direction[1, q, rows] - xi
            last_image[0, q, rows], last_image[1, q, rows] = lr, li
            halfway[0, q, rows], halfway[1, q, rows] = hr, hi
            dots[0] = dots[0] + lr * hr + li * hi
            dots[1] = dots[1] + lr * hi - li * hr
            dots[2] = dots[2] + lr * lr + li * li
    dots = [jnp.sum(t, axis=0, keepdims=True) for t in dots]
    row = lax.broadcasted_iota(jnp.int32, (8, ny), 0)
    alpha[...] = jnp.where(row == 0, ar, ai)

    for pair, found in enumerate(picks_of(corrected, ytable, xtable, qrow)):
        block = 0.0
        lines = [picks[2 * pair : 2 * pair + 1], picks[2 * pair + 1 : 2 * pair + 2]] + found + dots
        for k, line in enumerate(lines):
            block = jnp.where(row == k, line, block)
        pay[2 * pair] = block
        pay[2 * pair + 1] = block


def last_kernel(at, direction, corrected, last_image, halfway, alpha, got, solution, residual, pupil):
    group = got.shape[0]
    nx, ny = direction.shape[2:]
    total = got[0]
    for k in range(1, group):
        total = total + got[k]
    along_r, along_i, norm = [jnp.sum(total[k : k + 1], axis=1, keepdims=True) for k in (4, 5, 6)]
    wr = along_r / norm
    wi = along_i / norm
    ar = alpha[0:1, 0:1]
    ai = alpha[1:2, 0:1]
    for q in range(PLANES):
        for r0 in range(0, nx, CHUNK):
            rows = pl.ds(r0, CHUNK)
            xr, xi = cmul(ar, ai, direction[0, q, rows], direction[1, q, rows])
            yr, yi = cmul(wr, wi, corrected[0, q, rows], corrected[1, q, rows])
            solution[0, q, rows], solution[1, q, rows] = xr + yr, xi + yi
            zr, zi = cmul(wr, wi, last_image[0, q, rows], last_image[1, q, rows])
            residual[0, q, rows], residual[1, q, rows] = halfway[0, q, rows] - zr, halfway[1, q, rows] - zi
    tip = got[group - 1]
    xr, xi = cmul(ar, ai, tip[0:1], tip[1:2])
    yr, yi = cmul(wr, wi, tip[2:3], tip[3:4])
    both = jnp.concatenate([xr + yr, xi + yi] * 4, axis=0)
    both = jnp.where(at[1] == 1, pltpu.roll(both, ny // 2, 1), both)
    pupil[...] = both[:2, : ny // 2]


def exchange(x, mask, group):
    return lax.ppermute(x, "gz", [(i, i ^ mask) for i in range(group)])


def swap_across(x, group):
    pairs = []
    for i in range(1, group - 1, 2):
        pairs += [(i, i + 1), (i + 1, i)]
    return lax.ppermute(x, "gz", pairs)


def skip_across(x, group):
    pairs = []
    for i in range(group):
        target = i + 2 if i % 2 == 0 else i - 2
        if 0 <= target < group:
            pairs.append((i, target))
    return lax.ppermute(x, "gz", pairs)


def stages_of(group):
    stages = [[1]]
    stride = 2
    left = group // 2
    if left.bit_length() % 2 == 0:
        stages.insert(0, [stride])
        stride, left = 2 * stride, left // 2
    while left > 1:
        stages.insert(0, [stride, 2 * stride, 3 * stride])
        stride, left = 4 * stride, left // 4
    return stages


def gather(x, group):
    have, masks = x[None], [0]
    stages = stages_of(group)
    for masks_now in stages[:-1]:
        got = [exchange(have, m, group) for m in masks_now]
        masks = masks + [k ^ m for m in masks_now for k in masks]
        have = jnp.concatenate([have] + got, axis=0)
    (m,) = stages[-1]
    other = exchange(have, m, group)
    count = len(masks)
    layout = [(0, j) for j in range(count)] + [(1, j) for j in range(count)]
    return [have, other], masks + [k ^ m for k in masks], layout


def y_phases(nx, ny):
    q = np.arange(nx) - ORD_HALF
    turns = (q[:, None] * np.arange(ny)[None, :]) % ny
    angle = turns.astype(np.float64) * (2.0 * np.pi / ny)
    return np.concatenate([np.cos(angle), -np.sin(angle)], axis=0).astype(np.float32)


def on_device(source_term, material, orders):
    group = lax.axis_size("gz")
    _, planes, nx, ny = source_term.shape
    assert planes == PLANES and 2 * nx == ny and 2 * orders.shape[1] == ny
    me = lax.axis_index("gz")
    at = jnp.stack([me, me % 2, me * 0]).astype(jnp.int32)
    half = nx // 2

    fine = (2, PLANES, nx, ny)
    half_block = (3, OUTER, nx, ny)
    own, inner, outer = call(
        pack_kernel, [(3, PLANES, nx, ny), half_block, half_block], [at, source_term, material], []
    )
    swap = swap_across(inner, group)
    near = exchange(own, 1, group)
    swap_outer = swap_across(outer, group)
    skip = skip_across(outer, group)
    far = exchange(swap, 1, group)
    tall = nx + 2 * HALO
    (pay0,) = call(static_kernel, [(2 * half + half // 2 + 8, ny)], [at, own, orders], [(2, 2, nx, ny), (half, ny)])
    (pay1,) = call(
        first_kernel,
        [(4 * half + half // 2 + 8, ny)],
        [at, own, near, swap, pay0],
        [(2, 8, tall, ny), fine, (2, 8, tall, ny), (2, 2, nx, ny)],
    )
    gathered1, masks, layout = gather(pay1, group)
    window = (2, WINDOW, nx, ny)
    haloed = (2, WINDOW, tall, ny)
    shapes1 = (2 * group + 2 * PAD1, half, ny)
    shapes2 = (group + 2 * PAD2, half // 2, ny)
    f, weight, before, code = call(
        ahead_kernel, [window, window, haloed, (WINDOW, nx, ny)], [at, own, near, swap, swap_outer, skip, far], [haloed]
    )
    edge = (2, 2, nx, ny)
    direction, image, to_near, to_swap, pay2, w1r, w1i, w2r, w2i = call(
        functools.partial(second_kernel, masks, layout),
        [
            fine,
            (2, WINDOW - 8, nx, ny),
            edge,
            edge,
            (2 * half + 8, ny),
            shapes1,
            shapes1,
            shapes2,
            shapes2,
        ],
        [at, f, weight, before, code, *gathered1],
        [haloed, haloed, haloed, (2, 2, nx, ny), (WINDOW // 2, half, ny), window] + coarse_shapes(group, nx, ny),
    )
    near2 = exchange(to_near, 1, group)
    swap2 = swap_across(to_swap, group)
    wide, smooth2 = call(
        widen_kernel, [(2, 12, nx, ny), (2, 12, tall, ny)], [at, image, near2, swap2, weight], [(2, 12, tall, ny)]
    )
    ytable = jnp.asarray(y_phases(nx, ny))
    wanted = group * ny // 2
    xtable, qrow, picks = pl.pallas_call(
        functools.partial(phase_kernel, masks, layout, 4 * half + half // 2),
        out_shape=[
            jax.ShapeDtypeStruct((6 * nx, wanted), jnp.bfloat16),
            full((8, wanted)),
            full((group, ny)),
        ],
        in_specs=[SM] + [VM] * (2 + len(gathered1)),
        out_specs=[VM] * 3,
        scratch_shapes=[pltpu.VMEM((group, ny), F32)],
        compiler_params=pltpu.CompilerParams(vmem_limit_bytes=VMEM_LIMIT),
        cost_estimate=pl.CostEstimate(flops=4000000, bytes_accessed=600000, transcendentals=0),
        name="phases",
    )(at, ytable, direction, *gathered1)
    gathered2, masks, layout = gather(pay2, group)
    corrected, last_image, halfway, pay3, alpha = call(
        functools.partial(third_kernel, masks, layout),
        [fine, fine, fine, (group, 8, ny), (8, ny)],
        [
            at,
            own,
            direction,
            wide,
            smooth2,
            weight,
            w1r,
            w1i,
            w2r,
            w2i,
            ytable,
            xtable,
            qrow,
            picks,
            *gathered2,
        ],
        [(2, 12, tall, ny), (2, 12, tall, ny), (2, 2, nx, ny), (6, half, ny)] + coarse_shapes(group, nx, ny),
    )
    got = lax.all_to_all(pay3, "gz", 0, 0)
    solution, residual, pupil = call(
        last_kernel, [fine, fine, (2, ny // 2)], [at, direction, corrected, last_image, halfway, alpha, got], []
    )
    return solution, residual, pupil


def solution(mesh):
    return jax.shard_map(
        on_device,
        mesh=mesh,
        in_specs=(
            P(None, ("clip", "gz"), None, None),
            P(("clip", "gz"), None, None),
            P(None, "gz"),
        ),
        out_specs=(
            P(None, ("clip", "gz"), None, None),
            P(None, ("clip", "gz"), None, None),
            P(None, ("clip", "gz")),
        ),
        check_vma=False,
    )
```
